128 devices in a mesh: bins: 8 (over x_hi, y), tiles: 16 (over z, x_lo, core).
Axes of the slice: x: 4 (x_hi: 2, x_lo: 2; x = x_hi * 2 + x_lo), y: 4, z: 4, core: 2. Of those that a mesh axis runs over, the one named last changes fastest.
Arguments:
- spectrum: float32 [1152, 128, 1440], P('bins', 'tiles'), as said below
- sea_mask: int32 [128, 1440], P('tiles'), may hold values 0 or 1
- ice_mask: int32 [128, 1440], P('tiles'), may hold values 0 or 1
- friction: float32 [128, 1440], P('tiles'), may hold values from 0.2 to 1
- wind_dir: float32 [128, 1440], P('tiles'), may hold values from -3.140625 to 3.140625
- ocean_owner: int32 [16, 16], P('tiles'), may hold values from 0 to 7, as said below
Outputs:
- spectrum_next: float32 [1152, 128, 1440], P('bins', 'tiles')
- stokes_drift: float32 [2, 128, 16, 90], P(None, 'tiles', 'bins')
- wave_stress: float32 [2, 128, 16, 90], P(None, 'tiles', 'bins')
The draws below stay inside these ranges and needn't reach their ends.
Inputs may be any that keep to these rules, and one draw needn't show every extreme that they name: The spectrum is positive everywhere. `ocean_owner`: in every row each owner index appears exactly 2 times.
All inputs are finite; a program needn't handle non-finite values. No bound on the sum of `sea_mask` or of `ice_mask` on one device may be relied on, other than what follows from the above.
Results may differ from the reference program's by a relative error of at most 0.0001.
Values sent between devices are 32-bit elements; how exact they have to be, the bound alone decides.
No kernel may reach another device: no remote copies, remote signals or barrier semaphores. Data moves between devices by JAX's collectives and lax.ppermute only.
A program may use at most 192 MiB of HBM per device.

```python
import math
import jax
import jax.numpy as jnp
from jax import lax

NDIR = 36
NFREQ = 32
NBINS = 1152
LAT_DEV = 8
NLON = 1440
LON_BLOCKS = 16
BLK = 90
OWN_BLK = 2
NBANDS = 16
NLAT = 128
STEPS = 4


def draw_spectrum(key, part):
    noise = jax.random.uniform(key, (NDIR * NFREQ, NLAT, NLON), jnp.float32, -1.0, 1.0)
    freq_pos = (jnp.arange(NDIR * NFREQ) // NDIR).astype(jnp.float32)
    profile = jnp.power(1.03, NFREQ - 1 - freq_pos)[:, None, None]
    base = jnp.exp(1.2 * noise)
    return (0.05 * base * profile).astype(jnp.float32)


def shuffle_row(row_key):
    base = jnp.arange(LON_BLOCKS) // OWN_BLK
    return jax.random.permutation(row_key, base)


def draw_ocean_owner(key, part):
    row_keys = jax.random.split(key, NBANDS)
    return jax.vmap(shuffle_row)(row_keys).astype(jnp.int32)


def set_ends(array, stream_key, least, top_value):
    spot = [jax.random.randint(jax.random.fold_in(stream_key, axis), (), 0, length) for axis, length in enumerate(array.shape)]
    longest = array.shape.index(max(array.shape))
    next_to = spot[:longest] + [(spot[longest] + 1) % array.shape[longest]] + spot[longest + 1:]
    return array.at[tuple(spot)].set(least).at[tuple(next_to)].set(top_value)


def block_scale(stream_key, extent, cuts, smallest, top_value):
    def one(dim, shards_of):
        steps = jax.random.uniform(jax.random.fold_in(jax.random.fold_in(stream_key, 6), dim), (shards_of,), jnp.float32, smallest / len(cuts), top_value / len(cuts))
        return jnp.repeat(jnp.exp(steps), extent[dim] // shards_of).reshape((-1,) + (1,) * (len(extent) - dim - 1))

    factor_of = one(*cuts[0])
    for cut in cuts[1:]:
        factor_of = factor_of * one(*cut)
    return factor_of


def setup_inputs(seed: int = 0) -> dict:
    key_list = jax.random.split(jax.random.key(seed), 7)
    return {
        "spectrum": draw_spectrum(jax.random.fold_in(key_list[6], 71), 0),
        "sea_mask": set_ends((jax.random.randint(key_list[1], (NLAT, NLON), 0, 10) < 7).astype(jnp.int32), jax.random.fold_in(key_list[1], 1), 0, 1),
        "ice_mask": set_ends((jax.random.randint(key_list[2], (NLAT, NLON), 0, 6) < 1).astype(jnp.int32), jax.random.fold_in(key_list[2], 1), 0, 1),
        "friction": jnp.clip(jnp.exp(math.log(1.0) - 1.609438 * jax.random.uniform(key_list[3], (NLAT, NLON), jnp.float32) ** block_scale(key_list[3], (NLAT, NLON), ((0, 16),), -0.2, 0.2)), 0.2, 1.0),
        "wind_dir": jnp.clip(jax.random.uniform(key_list[4], (NLAT, NLON), jnp.float32, -3.140625, 3.140625), -3.140625, 3.140625),
        "ocean_owner": draw_ocean_owner(jax.random.fold_in(key_list[6], 71), 0),
    }


courant_max = 0.6
grid_step = 0.25 * math.pi / 180.0


def row_metric(first_row, count, lat_total):
    row_pos = (first_row + jnp.arange(count)).astype(jnp.float32)
    latitude = (row_pos - lat_total / 2 + 0.5) * grid_step
    edge_lat = (lat_total / 2 - 0.5) * grid_step
    return jnp.cos(jnp.asarray(edge_lat, jnp.float32)) / jnp.cos(latitude)


def advance(center, south_row, north_row, sea_open, courant_x, courant_y):
    west_cell = jnp.roll(center, 1, axis=2)
    east_cell = jnp.roll(center, -1, axis=2)
    result = center - jnp.maximum(courant_x, 0.0) * (center - west_cell)
    result = result - jnp.maximum(-courant_x, 0.0) * (center - east_cell)
    result = result - jnp.maximum(courant_y, 0.0) * (center - south_row)
    result = result - jnp.maximum(-courant_y, 0.0) * (center - north_row)
    return result * sea_open


def reference(spectrum, sea_mask, ice_mask, friction, wind_dir, ocean_owner):
    sea_open = sea_mask.astype(jnp.float32)
    ice_cover = ice_mask.astype(jnp.float32)
    metric = row_metric(0, NLAT, NLAT)
    angles = (jnp.arange(NDIR).astype(jnp.float32) + 0.5) * (2.0 * math.pi / NDIR)
    cos_dir = jnp.cos(angles)[:, None, None]
    sin_dir = jnp.sin(angles)[:, None, None]
    alignment = jnp.maximum(jnp.cos(angles[:, None, None] - wind_dir[None]), 0.0)
    blocks = spectrum.reshape(NFREQ, NDIR, NLAT, NLON)

    def advance_freq(totals, scan_item):
        freq_index, spectral = scan_item
        freq_pos = freq_index.astype(jnp.float32)
        speed_ratio = jnp.power(1.1, -freq_pos)
        freq_weight = jnp.power(1.03, freq_pos - (NFREQ - 1))
        courant_x = courant_max * speed_ratio * cos_dir * metric[None, :, None]
        courant_y = courant_max * speed_ratio * sin_dir
        spectral = spectral * sea_open
        for sub_step in range(STEPS):
            padded = jnp.pad(spectral, ((0, 0), (1, 1), (0, 0)))
            spectral = advance(spectral, padded[:, :-2], padded[:, 2:], sea_open, courant_x, courant_y)
        growth = 0.5 * friction[None] ** 2 * freq_weight * alignment
        source = growth * spectral
        updated = (spectral + source) * (1.0 - 0.5 * ice_cover)
        partial_value = jnp.stack([
            jnp.sum(freq_weight * cos_dir * updated, axis=0),
            jnp.sum(freq_weight * sin_dir * updated, axis=0),
            jnp.sum(cos_dir * source, axis=0),
            jnp.sum(sin_dir * source, axis=0)])
        return totals + partial_value, updated

    start = jnp.zeros((4, NLAT, NLON), jnp.float32)
    totals, updated = lax.scan(advance_freq, start, (jnp.arange(NFREQ).astype(jnp.int32), blocks))
    spectrum_next = updated.reshape(NBINS, NLAT, NLON)
    fields = totals.reshape(4, NLAT, LON_BLOCKS, BLK)
    ocean_order = jnp.argsort(ocean_owner, axis=1, stable=True).astype(jnp.int32)
    row_order = jnp.repeat(ocean_order, LAT_DEV, axis=0)
    ocean_fields = jnp.take_along_axis(fields, row_order[None, :, :, None], axis=2)
    return spectrum_next, ocean_fields[:2], ocean_fields[2:]
```

```python
import math

import jax
import jax.numpy as jnp
from jax import lax
from jax.experimental import pallas as pl
from jax.experimental.pallas import tpu as pltpu
from jax.sharding import PartitionSpec as P

NDIR = 36
NFREQ = 32
LON_BLOCKS = 16
STEPS = 4
COURANT_MAX = 0.6
GRID_STEP = 0.25 * math.pi / 180.0

ROWS = 8
NLON = 1440
BLK = 90
LANES = 128
TILES = 12
TAIL = NLON - (TILES - 1) * LANES
NF = 4
GROUPS = 9
G1 = 7
G2 = GROUPS - G1
TPG = NF * (TILES - 1) + 1

F32 = jnp.float32
OFF_BX = 0
OFF_BY = NF * NDIR
OFF_COS = 2 * NF * NDIR
OFF_SIN = OFF_COS + NDIR
OFF_P = OFF_SIN + NDIR


def lane_iota():
    return lax.broadcasted_iota(jnp.int32, (ROWS, LANES), 1)


def sub_iota():
    return lax.broadcasted_iota(jnp.int32, (ROWS, LANES), 0)


def pack_group(src_ref, mask_ref, out_ref, upward, lane, low):
    def pair(j, i):
        cols = pl.ds(i * LANES, LANES)
        first = src_ref[j, 0, :, cols]
        second = src_ref[j, 1, :, cols]
        mask = mask_ref[:, cols].astype(F32)
        first = first * mask
        second = second * mask
        if upward:
            return jnp.where(low, pltpu.roll(first, 4, 0), second)
        return jnp.where(low, first, pltpu.roll(second, 4, 0))

    for i in range(TILES - 1):
        for j in range(NF):
            out_ref[0, j * (TILES - 1) + i] = pair(j, i)
    tail = pair(0, TILES - 1)
    for j in range(1, NF):
        moved = pltpu.roll(pair(j, TILES - 1), TAIL * j, 1)
        tail = jnp.where(lane >= TAIL * j, moved, tail)
    out_ref[0, TPG - 1] = tail


def pack_kernel(with_mask, south_ref, north_ref, mask_ref, up_ref, dn_ref):
    lane = lane_iota()
    low = sub_iota() < 4
    pack_group(south_ref, mask_ref, up_ref, True, lane, low)
    pack_group(north_ref, mask_ref, dn_ref, False, lane, low)
    if with_mask:
        start = jnp.minimum(pl.program_id(0), TILES // 2 - 1) * (2 * LANES)
        start = pl.multiple_of(start, 2 * LANES)
        first = mask_ref[:, pl.ds(start, LANES)].astype(F32)
        second = mask_ref[:, pl.ds(start + LANES, LANES)].astype(F32)
        up_ref[0, TPG] = jnp.where(low, pltpu.roll(first, 4, 0), second)
        dn_ref[0, TPG] = jnp.where(low, first, pltpu.roll(second, 4, 0))


def pack(spectral, sea_mask, base, groups, with_mask):
    tiles = TPG + 1 if with_mask else TPG
    block = (NF, 2, ROWS, TILES * LANES)
    out = jax.ShapeDtypeStruct((groups, tiles, ROWS, LANES), F32)
    out_spec = pl.BlockSpec((1, tiles, ROWS, LANES), lambda g: (g, 0, 0, 0))
    return pl.pallas_call(
        lambda *refs: pack_kernel(with_mask, *refs),
        grid=(groups,),
        in_specs=[
            pl.BlockSpec(block, lambda g: (0, base + g, 0, 0)),
            pl.BlockSpec(block, lambda g: (0, 2 * GROUPS - 1 - base - g, 0, 0)),
            pl.BlockSpec((ROWS, TILES * LANES), lambda g: (0, 0)),
        ],
        out_specs=[out_spec, out_spec],
        out_shape=[out, out],
        name="pack%d" % base,
    )(spectral, spectral, sea_mask)


def fill_wrap(tiles, west, lane):
    last = tiles[-1]
    if west:
        moved = pltpu.roll(last, LANES - TAIL, 1)
    else:
        moved = pltpu.roll(tiles[0], TAIL, 1)
    return tiles[:-1] + [jnp.where(lane < TAIL, last, moved)]


def advance(tiles, mask_at, alpha, cx, cy, west, south, lane):
    shift = 1 if west else LANES - 1
    edge = (lane == 0) if west else (lane == LANES - 1)
    for step in range(STEPS):
        moved = [pltpu.roll(t, shift, 1) for t in tiles]
        new = []
        for i in range(TILES):
            near = moved[i - 1] if west else moved[(i + 1) % TILES]
            x = jnp.where(edge, near, moved[i])
            y = pltpu.roll(tiles[i], 1 if south else ROWS - 1, 0)
            new.append((alpha * tiles[i] + cx * x + cy * y) * mask_at(i))
        tiles = new
    return tiles


def variants(dp, dd, body):
    direction = 2 * dp + dd
    is_south = dp < GROUPS
    is_west = jnp.logical_or(direction < NDIR // 4, direction >= NDIR - NDIR // 4)
    for south in (True, False):
        for west in (True, False):
            cond = jnp.logical_and(is_south == south, is_west == west)
            pl.when(cond)(lambda west=west, south=south: body(west, south))


def own_kernel(tab_ref, met_ref, mask_ref, src_ref, out_ref):
    dp = pl.program_id(0)
    lane = lane_iota()
    low = sub_iota() < 4
    for dd in range(2):

        def body(west, south, dd=dd):
            def one(j, carry):
                index = j * NDIR + 2 * dp + dd
                cy = tab_ref[OFF_BY + index]
                cx = tab_ref[OFF_BX + index] * met_ref[0]
                alpha = 1.0 - cx - cy
                start = [
                    src_ref[j, dd, :, pl.ds(i * LANES, LANES)] for i in range(TILES)
                ]
                start = fill_wrap(start, west, lane)
                start = [t * mask_ref[i] for i, t in enumerate(start)]
                done = advance(
                    start, lambda i: mask_ref[i], alpha, cx, cy, west, south, lane
                )
                for i in range(TILES):
                    if south:
                        kept = jnp.where(low, start[i], done[i])
                    else:
                        kept = jnp.where(low, done[i], start[i])
                    out_ref[0, dd, j, i] = kept
                return carry

            lax.fori_loop(0, NF, one, 0)

        variants(dp, dd, body)


def own_rows(spectral, table, metric, mask):
    whole = pl.BlockSpec(memory_space=pltpu.VMEM)
    return pl.pallas_call(
        own_kernel,
        grid=(2 * GROUPS,),
        in_specs=[
            pl.BlockSpec(memory_space=pltpu.SMEM),
            whole,
            whole,
            pl.BlockSpec((NF, 2, ROWS, TILES * LANES), lambda d: (0, d, 0, 0)),
        ],
        out_specs=pl.BlockSpec(
            (1, 2, NF, TILES, ROWS, LANES), lambda d: (d, 0, 0, 0, 0, 0)
        ),
        out_shape=jax.ShapeDtypeStruct((2 * GROUPS, 2, NF, TILES, ROWS, LANES), F32),
        name="own",
    )(table, metric, mask, spectral)


def finish_kernel(
    dp_of,
    first,
    tab_ref,
    met_ref,
    mask_ref,
    wind_ref,
    own_ref,
    up_ref,
    dn_ref,
    prev_ref,
    old_ref,
    out_ref,
    acc_ref,
    e_ref,
):
    step = pl.program_id(0)
    dp = dp_of(step)
    lane = lane_iota()
    low = sub_iota() < 4

    @pl.when(step == 0)
    def _():
        if first:
            acc_ref[...] = jnp.zeros_like(acc_ref)
        else:
            acc_ref[...] = prev_ref[...]

    for dd in range(2):

        def body(west, south, dd=dd):
            halo_ref = up_ref if south else dn_ref
            side = 0 if south else 1
            swap = (dd == 0) if south else (dd == 1)

            def one(j, carry):
                index = j * NDIR + 2 * dp + dd
                cy = tab_ref[OFF_BY + index]
                cx = tab_ref[OFF_BX + index] * met_ref[1 + side]
                alpha = 1.0 - cx - cy
                start = []
                own = []
                for i in range(TILES):
                    if i < TILES - 1:
                        halo = halo_ref[0, j * (TILES - 1) + i]
                    else:
                        halo = pltpu.roll(
                            halo_ref[0, TPG - 1], (LANES - TAIL * j) % LANES, 1
                        )
                    if swap:
                        halo = pltpu.roll(halo, 4, 0)
                    mine = own_ref[0, dd, j, i]
                    own.append(mine)
                    if south:
                        start.append(jnp.where(low, mine, halo))
                    else:
                        start.append(jnp.where(low, halo, mine))
                start = fill_wrap(start, west, lane)
                done = advance(
                    start,
                    lambda i: mask_ref[side, i],
                    alpha,
                    cx,
                    cy,
                    west,
                    south,
                    lane,
                )
                for i in range(TILES):
                    if south:
                        e_ref[j, i] = jnp.where(low, done[i], own_ref[0, dd, j, i])
                    else:
                        e_ref[j, i] = jnp.where(low, own_ref[0, dd, j, i], done[i])
                return carry

            lax.fori_loop(0, NF, one, 0)

        variants(dp, dd, body)
        cos_d = tab_ref[OFF_COS + 2 * dp + dd]
        sin_d = tab_ref[OFF_SIN + 2 * dp + dd]
        weight = [tab_ref[OFF_P + j] for j in range(NF)]
        for i in range(TILES):
            h = jnp.maximum(cos_d * wind_ref[0, i] + sin_d * wind_ref[1, i], 0.0)
            ice = wind_ref[2, i]
            for j in range(NF):
                e = e_ref[j, i]
                x = weight[j] * e
                out_ref[j, dd, :, pl.ds(i * LANES, LANES)] = (e + h * x) * ice
                y = weight[j] * x
                sum_x = x if j == 0 else sum_x + x
                sum_y = y if j == 0 else sum_y + y
            source = h * sum_x
            drift = ice * (sum_x + h * sum_y)
            acc_ref[0, i] += cos_d * drift
            acc_ref[1, i] += sin_d * drift
            acc_ref[2, i] += cos_d * source
            acc_ref[3, i] += sin_d * source


def finish(table, metric, masks, wind, own, up, dn, prev, old, base):
    first = prev is None
    groups = up.shape[0]
    if first:
        dp_of = lambda i: jnp.where(i < groups, i, i + 2 * (GROUPS - groups))
    else:
        dp_of = lambda i: i + base
    tiles = up.shape[1]
    whole = pl.BlockSpec(memory_space=pltpu.VMEM)
    anywhere = pl.BlockSpec(memory_space=pl.ANY)
    acc = jax.ShapeDtypeStruct((4, TILES, ROWS, LANES), F32)
    out = jax.ShapeDtypeStruct((NF, NDIR, ROWS, NLON), F32)
    in_specs = [
        pl.BlockSpec(memory_space=pltpu.SMEM),
        whole,
        whole,
        whole,
        pl.BlockSpec(
            (1, 2, NF, TILES, ROWS, LANES), lambda i: (dp_of(i), 0, 0, 0, 0, 0)
        ),
        pl.BlockSpec(
            (1, tiles, ROWS, LANES), lambda i: (jnp.minimum(i, groups - 1), 0, 0, 0)
        ),
        pl.BlockSpec(
            (1, tiles, ROWS, LANES),
            lambda i: (jnp.minimum(2 * groups - 1 - i, groups - 1), 0, 0, 0),
        ),
    ]
    args = [table, metric, masks, wind, own, up, dn]
    aliases = {}
    if first:
        kernel = lambda *r: finish_kernel(dp_of, True, *r[:7], None, None, *r[7:])
    else:
        kernel = lambda *r: finish_kernel(dp_of, False, *r)
        in_specs += [whole, anywhere]
        args += [prev, old]
        aliases = {8: 0}
    return pl.pallas_call(
        kernel,
        grid=(2 * groups,),
        in_specs=in_specs,
        out_specs=[
            pl.BlockSpec(
                (NF, 2, ROWS, TILES * LANES), lambda i: (0, dp_of(i), 0, 0)
            ),
            pl.BlockSpec((4, TILES, ROWS, LANES), lambda i: (0, 0, 0, 0)),
        ],
        out_shape=[out, acc],
        scratch_shapes=[pltpu.VMEM((NF, TILES, ROWS, LANES), F32)],
        input_output_aliases=aliases,
        name="finish%d" % base,
    )(*args)


def slots_kernel(order_ref, acc_ref, out_ref):
    lane = lane_iota()

    def owner(k, carry):
        rests = []
        for c in range(4):
            parts = []
            for s in range(2):
                column = order_ref[2 * k + s] * BLK
                tile = column // LANES
                shift = column % LANES
                back = (LANES - shift) % LANES
                here = pltpu.roll(acc_ref[c, tile], back, 1)
                after = pltpu.roll(acc_ref[c, jnp.minimum(tile + 1, TILES - 1)], back, 1)
                parts.append(jnp.where(lane < LANES - shift, here, after))
            moved = pltpu.roll(parts[1], BLK, 1)
            out_ref[k, c] = jnp.where(lane < BLK, parts[0], moved)
            rests.append(moved)
        for c in range(2):
            other = pltpu.roll(rests[2 * c + 1], LANES // 2, 1)
            both = jnp.where(lane < LANES // 2, rests[2 * c], other)
            used = lane % (LANES // 2) < 2 * BLK - LANES
            out_ref[k, 4 + c] = jnp.where(used, both, 0.0)
        return carry

    lax.fori_loop(0, LON_BLOCKS // 2, owner, 0)


def pick_slots(order, acc):
    return pl.pallas_call(
        slots_kernel,
        in_specs=[
            pl.BlockSpec(memory_space=pltpu.SMEM),
            pl.BlockSpec(memory_space=pltpu.VMEM),
        ],
        out_specs=pl.BlockSpec(memory_space=pltpu.VMEM),
        out_shape=jax.ShapeDtypeStruct((LON_BLOCKS // 2, 6, ROWS, LANES), F32),
        name="slots",
    )(order, acc)


def as_tiles(field):
    return field.reshape(ROWS, TILES, LANES).transpose(1, 0, 2)


def with_wrap(field):
    side = (TILES * LANES - NLON) // 2
    return jnp.concatenate([field, field[:, :side], field[:, NLON - side :]], axis=1)


def edge_mask(received):
    tiles = received[: TILES // 2, TPG].reshape(TILES, 4, LANES)
    return tiles.transpose(1, 0, 2).reshape(4, TILES * LANES)[:, :NLON]


def row_metric(row_pos, lat_total):
    latitude = (row_pos.astype(F32) - lat_total / 2 + 0.5) * GRID_STEP
    edge_lat = (lat_total / 2 - 0.5) * GRID_STEP
    return jnp.cos(jnp.asarray(edge_lat, F32)) / jnp.cos(latitude)


def shards(spectrum, sea_mask, ice_mask, friction, wind_dir, ocean_owner):
    count = lax.axis_size("tiles")
    first_row = lax.axis_index("tiles") * ROWS
    up_pairs = [(i, i + 1) for i in range(count - 1)]
    dn_pairs = [(i + 1, i) for i in range(count - 1)]
    spectral = spectrum.reshape(NF, NDIR, ROWS, NLON)

    up1, dn1 = pack(spectral, sea_mask, 0, G1, True)
    up1 = lax.ppermute(up1, "tiles", up_pairs)
    dn1 = lax.ppermute(dn1, "tiles", dn_pairs)
    up2, dn2 = pack(spectral, sea_mask, G1, G2, False)
    up2 = lax.ppermute(up2, "tiles", up_pairs)
    dn2 = lax.ppermute(dn2, "tiles", dn_pairs)

    freq_pos = (lax.axis_index("bins") * NF + jnp.arange(NF)).astype(F32)
    speed_ratio = jnp.power(1.1, -freq_pos)
    freq_weight = jnp.power(1.03, freq_pos - (NFREQ - 1))
    angles = (jnp.arange(NDIR).astype(F32) + 0.5) * (2.0 * math.pi / NDIR)
    cos_dir = jnp.cos(angles)
    sin_dir = jnp.sin(angles)
    courant = (COURANT_MAX * speed_ratio)[:, None]
    table = jnp.concatenate(
        [
            (courant * jnp.abs(cos_dir)).reshape(-1),
            (courant * jnp.abs(sin_dir)).reshape(-1),
            cos_dir,
            sin_dir,
            freq_weight,
        ]
    )
    sub = jnp.arange(ROWS)
    rows = jnp.stack(
        [sub, jnp.where(sub < 4, sub, sub - ROWS), jnp.where(sub < 4, sub + ROWS, sub)]
    )
    metric = row_metric(first_row + rows, ROWS * count)
    metric = jnp.broadcast_to(metric[:, :, None], (3, ROWS, LANES))

    sea = sea_mask.astype(F32)
    mask = as_tiles(with_wrap(sea))
    strength = 0.5 * friction**2
    wind = jnp.stack(
        [
            strength * jnp.cos(wind_dir),
            strength * jnp.sin(wind_dir),
            1.0 - 0.5 * ice_mask.astype(F32),
        ]
    )
    wind = jnp.pad(wind, ((0, 0), (0, 0), (0, TILES * LANES - NLON)))
    wind = wind.reshape(3, ROWS, TILES, LANES).transpose(0, 2, 1, 3)
    order = jnp.argsort(ocean_owner[0], stable=True).astype(jnp.int32)

    own = own_rows(spectral, table, metric, mask)

    south = jnp.concatenate([sea[:4], edge_mask(up1)], axis=0)
    north = jnp.concatenate([edge_mask(dn1), sea[4:]], axis=0)
    masks = jnp.stack([as_tiles(with_wrap(south)), as_tiles(with_wrap(north))])

    out, acc = finish(table, metric, masks, wind, own, up1, dn1, None, None, 0)
    out, acc = finish(table, metric, masks, wind, own, up2, dn2, acc, out, G1)

    sent = pick_slots(order, acc)
    got = lax.all_to_all(sent, "bins", 0, 0, tiled=True)
    total = got.sum(0)
    rest = total[4:].reshape(2, ROWS, 2, LANES // 2).transpose(0, 2, 1, 3)
    rest = rest.reshape(4, ROWS, LANES // 2)[:, :, : 2 * BLK - LANES]
    fields = jnp.concatenate([total[:4], rest], axis=2).reshape(4, ROWS, 2, BLK)
    return out.reshape(spectrum.shape), fields[:2], fields[2:]


def solution(mesh):
    field = P("tiles", None)
    blocks = P(None, "tiles", "bins", None)
    whole = P("bins", "tiles", None)
    return jax.shard_map(
        shards,
        mesh=mesh,
        in_specs=(whole, field, field, field, field, field),
        out_specs=(whole, blocks, blocks),
        check_vma=False,
    )
```

```python
import math

import jax
import jax.numpy as jnp
from jax import lax
from jax.experimental import pallas as pl
from jax.experimental.pallas import tpu as pltpu
from jax.sharding import PartitionSpec as P

NDIR = 36
NFREQ = 32
LON_BLOCKS = 16
STEPS = 4
COURANT_MAX = 0.6
GRID_STEP = 0.25 * math.pi / 180.0

ROWS = 8
NLON = 1440
BLK = 90
LANES = 128
TILES = 12
TAIL = NLON - (TILES - 1) * LANES
NF = 4
GROUPS = 9
G1 = 7
G2 = GROUPS - G1
TPG = NF * (TILES - 1) + 1

F32 = jnp.float32
LIMIT = 12 << 20
OFF_BX = 0
OFF_BY = NF * NDIR
OFF_COS = 2 * NF * NDIR
OFF_SIN = OFF_COS + NDIR
OFF_P = OFF_SIN + NDIR


def lane_iota():
    return lax.broadcasted_iota(jnp.int32, (ROWS, LANES), 1)


def sub_iota():
    return lax.broadcasted_iota(jnp.int32, (ROWS, LANES), 0)


def pack_group(src_ref, mask_ref, out_ref, g, upward, lane, low):
    def pair(j, i):
        cols = pl.ds(i * LANES, LANES)
        first = src_ref[j, 0, :, cols]
        second = src_ref[j, 1, :, cols]
        mask = mask_ref[:, cols].astype(F32)
        first = first * mask
        second = second * mask
        if upward:
            return jnp.where(low, pltpu.roll(first, 4, 0), second)
        return jnp.where(low, first, pltpu.roll(second, 4, 0))

    for i in range(TILES - 1):
        for j in range(NF):
            out_ref[g, j * (TILES - 1) + i] = pair(j, i)
    tail = pair(0, TILES - 1)
    for j in range(1, NF):
        moved = pltpu.roll(pair(j, TILES - 1), TAIL * j, 1)
        tail = jnp.where(lane >= TAIL * j, moved, tail)
    out_ref[g, TPG - 1] = tail


def pack_kernel(with_mask, south_ref, north_ref, mask_ref, up_ref, dn_ref):
    g = pl.program_id(0)
    lane = lane_iota()
    low = sub_iota() < 4
    pack_group(south_ref, mask_ref, up_ref, g, True, lane, low)
    pack_group(north_ref, mask_ref, dn_ref, g, False, lane, low)
    if with_mask:
        start = jnp.minimum(g, TILES // 2 - 1) * (2 * LANES)
        start = pl.multiple_of(start, 2 * LANES)
        first = mask_ref[:, pl.ds(start, LANES)].astype(F32)
        second = mask_ref[:, pl.ds(start + LANES, LANES)].astype(F32)
        up_ref[g, TPG] = jnp.where(low, pltpu.roll(first, 4, 0), second)
        dn_ref[g, TPG] = jnp.where(low, first, pltpu.roll(second, 4, 0))


def pack(spectral, sea_mask, base, groups, with_mask):
    tiles = TPG + 1 if with_mask else TPG
    block = (NF, 2, ROWS, TILES * LANES)
    out = pltpu.VMEM((groups, tiles, ROWS, LANES), F32)
    out_spec = pl.BlockSpec(memory_space=pltpu.VMEM)
    return pl.pallas_call(
        lambda *refs: pack_kernel(with_mask, *refs),
        grid=(groups,),
        in_specs=[
            pl.BlockSpec(block, lambda g: (0, base + g, 0, 0)),
            pl.BlockSpec(block, lambda g: (0, 2 * GROUPS - 1 - base - g, 0, 0)),
            pl.BlockSpec((ROWS, TILES * LANES), lambda g: (0, 0)),
        ],
        out_specs=[out_spec, out_spec],
        out_shape=[out, out],
        compiler_params=pltpu.CompilerParams(vmem_limit_bytes=LIMIT),
        name="pack%d" % base,
    )(spectral, spectral, sea_mask)


def fill_wrap(tiles, west, lane):
    last = tiles[-1]
    if west:
        moved = pltpu.roll(last, LANES - TAIL, 1)
    else:
        moved = pltpu.roll(tiles[0], TAIL, 1)
    return tiles[:-1] + [jnp.where(lane < TAIL, last, moved)]


def advance(bins, mask_at, west, south, lane):
    shift = 1 if west else LANES - 1
    edge = (lane == 0) if west else (lane == LANES - 1)
    fields = [b[0] for b in bins]
    for step in range(STEPS):
        moved = [[pltpu.roll(t, shift, 1) for t in tiles] for tiles in fields]
        new = []
        for tiles, shifted, (_, alpha, cx, cy) in zip(fields, moved, bins):
            done = []
            for i in range(TILES):
                near = shifted[i - 1] if west else shifted[(i + 1) % TILES]
                x = jnp.where(edge, near, shifted[i])
                y = pltpu.roll(tiles[i], 1 if south else ROWS - 1, 0)
                done.append((alpha * tiles[i] + cx * x + cy * y) * mask_at(i))
            new.append(done)
        fields = new
    return fields


def variants(dp, dd, body):
    direction = 2 * dp + dd
    is_south = dp < GROUPS
    is_west = jnp.logical_or(direction < NDIR // 4, direction >= NDIR - NDIR // 4)
    for south in (True, False):
        for west in (True, False):
            cond = jnp.logical_and(is_south == south, is_west == west)
            pl.when(cond)(lambda west=west, south=south: body(west, south))


def own_kernel(tab_ref, met_ref, mask_ref, src_ref, out_ref):
    dp = pl.program_id(0)
    lane = lane_iota()
    low = sub_iota() < 4
    for dd in range(2):

        def body(west, south, dd=dd):
            bins = []
            for j in range(NF):
                index = j * NDIR + 2 * dp + dd
                cy = tab_ref[OFF_BY + index]
                cx = tab_ref[OFF_BX + index] * met_ref[0]
                start = [
                    src_ref[j, dd, :, pl.ds(i * LANES, LANES)] for i in range(TILES)
                ]
                start = fill_wrap(start, west, lane)
                start = [t * mask_ref[i] for i, t in enumerate(start)]
                bins.append((start, 1.0 - cx - cy, cx, cy))
            fields = advance(bins, lambda i: mask_ref[i], west, south, lane)
            for j in range(NF):
                for i in range(TILES):
                    first, last = bins[j][0][i], fields[j][i]
                    if not south:
                        first, last = last, first
                    out_ref[dp, dd, j, i] = jnp.where(low, first, last)

        variants(dp, dd, body)


def own_rows(spectral, table, metric, mask):
    whole = pl.BlockSpec(memory_space=pltpu.VMEM)
    return pl.pallas_call(
        own_kernel,
        grid=(2 * GROUPS,),
        in_specs=[
            pl.BlockSpec(memory_space=pltpu.SMEM),
            whole,
            whole,
            pl.BlockSpec((NF, 2, ROWS, TILES * LANES), lambda d: (0, d, 0, 0)),
        ],
        out_specs=whole,
        out_shape=pltpu.VMEM((2 * GROUPS, 2, NF, TILES, ROWS, LANES), F32),
        compiler_params=pltpu.CompilerParams(vmem_limit_bytes=LIMIT),
        name="own",
    )(table, metric, mask, spectral)


def finish_kernel(
    dp_of,
    first,
    tab_ref,
    met_ref,
    mask_ref,
    wind_ref,
    own_ref,
    up_ref,
    dn_ref,
    prev_ref,
    old_ref,
    out_ref,
    acc_ref,
    e_ref,
):
    step = pl.program_id(0)
    dp = dp_of(step)
    groups = up_ref.shape[0]
    group = jnp.where(step < groups, step, 2 * groups - 1 - step)
    lane = lane_iota()
    low = sub_iota() < 4

    @pl.when(step == 0)
    def _():
        if first:
            acc_ref[...] = jnp.zeros_like(acc_ref)
        else:
            acc_ref[...] = prev_ref[...]

    for dd in range(2):

        def body(west, south, dd=dd):
            halo_ref = up_ref if south else dn_ref
            side = 0 if south else 1
            swap = (dd == 0) if south else (dd == 1)

            bins = []
            for j in range(NF):
                index = j * NDIR + 2 * dp + dd
                cy = tab_ref[OFF_BY + index]
                cx = tab_ref[OFF_BX + index] * met_ref[1 + side]
                start = []
                for i in range(TILES):
                    if i < TILES - 1:
                        halo = halo_ref[group, j * (TILES - 1) + i]
                    else:
                        halo = halo_ref[group, TPG - 1]
                        if j > 0:
                            halo = pltpu.roll(halo, LANES - TAIL * j, 1)
                    if swap:
                        halo = pltpu.roll(halo, 4, 0)
                    mine = own_ref[dp, dd, j, i]
                    if south:
                        start.append(jnp.where(low, mine, halo))
                    else:
                        start.append(jnp.where(low, halo, mine))
                start = fill_wrap(start, west, lane)
                bins.append((start, 1.0 - cx - cy, cx, cy))
            fields = advance(bins, lambda i: mask_ref[side, i], west, south, lane)
            for j in range(NF):
                for i in range(TILES):
                    first, last = fields[j][i], own_ref[dp, dd, j, i]
                    if not south:
                        first, last = last, first
                    e_ref[j, i] = jnp.where(low, first, last)

        variants(dp, dd, body)
        cos_d = tab_ref[OFF_COS + 2 * dp + dd]
        sin_d = tab_ref[OFF_SIN + 2 * dp + dd]
        weight = [tab_ref[OFF_P + j] for j in range(NF)]
        for i in range(TILES):
            h = jnp.maximum(cos_d * wind_ref[0, i] + sin_d * wind_ref[1, i], 0.0)
            ice = wind_ref[2, i]
            for j in range(NF):
                e = e_ref[j, i]
                x = weight[j] * e
                out_ref[j, dd, :, pl.ds(i * LANES, LANES)] = (e + h * x) * ice
                y = weight[j] * x
                sum_x = x if j == 0 else sum_x + x
                sum_y = y if j == 0 else sum_y + y
            source = h * sum_x
            drift = ice * (sum_x + h * sum_y)
            acc_ref[0, i] += cos_d * drift
            acc_ref[1, i] += sin_d * drift
            acc_ref[2, i] += cos_d * source
            acc_ref[3, i] += sin_d * source


def in_vmem(x):
    return pltpu.with_memory_space_constraint(x, pltpu.VMEM)


def finish(table, metric, masks, wind, own, up, dn, prev, old, base):
    first = prev is None
    groups = up.shape[0]
    if first:
        dp_of = lambda i: jnp.where(i < groups, i, i + 2 * (GROUPS - groups))
    else:
        dp_of = lambda i: i + base
    whole = pl.BlockSpec(memory_space=pltpu.VMEM)
    anywhere = pl.BlockSpec(memory_space=pl.ANY)
    acc = pltpu.VMEM((4, TILES, ROWS, LANES), F32)
    out = jax.ShapeDtypeStruct((NF, NDIR, ROWS, NLON), F32)
    in_specs = [
        pl.BlockSpec(memory_space=pltpu.SMEM),
        whole,
        whole,
        whole,
        whole,
        whole,
        whole,
    ]
    args = [table, metric, masks, wind, in_vmem(own), in_vmem(up), in_vmem(dn)]
    aliases = {}
    if first:
        kernel = lambda *r: finish_kernel(dp_of, True, *r[:7], None, None, *r[7:])
    else:
        kernel = lambda *r: finish_kernel(dp_of, False, *r)
        in_specs += [whole, anywhere]
        args += [prev, old]
        aliases = {8: 0}
    return pl.pallas_call(
        kernel,
        grid=(2 * groups,),
        in_specs=in_specs,
        out_specs=[
            pl.BlockSpec(
                (NF, 2, ROWS, TILES * LANES), lambda i: (0, dp_of(i), 0, 0)
            ),
            whole,
        ],
        out_shape=[out, acc],
        scratch_shapes=[pltpu.VMEM((NF, TILES, ROWS, LANES), F32)],
        input_output_aliases=aliases,
        compiler_params=pltpu.CompilerParams(vmem_limit_bytes=LIMIT),
        name="finish%d" % base,
    )(*args)


def slots_kernel(order_ref, acc_ref, out_ref):
    lane = lane_iota()

    for k in range(LON_BLOCKS // 2):
        rests = []
        for c in range(4):
            parts = []
            for s in range(2):
                column = order_ref[2 * k + s] * BLK
                tile = column // LANES
                shift = column % LANES
                back = (LANES - shift) % LANES
                here = pltpu.roll(acc_ref[c, tile], back, 1)
                after = pltpu.roll(acc_ref[c, jnp.minimum(tile + 1, TILES - 1)], back, 1)
                parts.append(jnp.where(lane < LANES - shift, here, after))
            moved = pltpu.roll(parts[1], BLK, 1)
            out_ref[k, c] = jnp.where(lane < BLK, parts[0], moved)
            rests.append(moved)
        for c in range(2):
            other = pltpu.roll(rests[2 * c + 1], LANES // 2, 1)
            both = jnp.where(lane < LANES // 2, rests[2 * c], other)
            used = lane % (LANES // 2) < 2 * BLK - LANES
            out_ref[k, 4 + c] = jnp.where(used, both, 0.0)


def pick_slots(order, acc):
    return pl.pallas_call(
        slots_kernel,
        in_specs=[
            pl.BlockSpec(memory_space=pltpu.SMEM),
            pl.BlockSpec(memory_space=pltpu.VMEM),
        ],
        out_specs=pl.BlockSpec(memory_space=pltpu.VMEM),
        out_shape=pltpu.VMEM((LON_BLOCKS // 2, 6, ROWS, LANES), F32),
        compiler_params=pltpu.CompilerParams(vmem_limit_bytes=LIMIT),
        name="slots",
    )(order, acc)


def as_tiles(field):
    return field.reshape(ROWS, TILES, LANES).transpose(1, 0, 2)


def with_wrap(field):
    side = (TILES * LANES - NLON) // 2
    return jnp.concatenate([field, field[:, :side], field[:, NLON - side :]], axis=1)


def edge_mask(received):
    tiles = received[: TILES // 2, TPG].reshape(TILES, 4, LANES)
    return tiles.transpose(1, 0, 2).reshape(4, TILES * LANES)[:, :NLON]


def row_metric(row_pos, lat_total):
    latitude = (row_pos.astype(F32) - lat_total / 2 + 0.5) * GRID_STEP
    edge_lat = (lat_total / 2 - 0.5) * GRID_STEP
    return jnp.cos(jnp.asarray(edge_lat, F32)) / jnp.cos(latitude)


def shards(spectrum, sea_mask, ice_mask, friction, wind_dir, ocean_owner):
    count = lax.axis_size("tiles")
    first_row = lax.axis_index("tiles") * ROWS
    up_pairs = [(i, i + 1) for i in range(count - 1)]
    dn_pairs = [(i + 1, i) for i in range(count - 1)]
    spectral = spectrum.reshape(NF, NDIR, ROWS, NLON)

    up1, dn1 = pack(spectral, sea_mask, 0, G1, True)
    up1 = lax.ppermute(up1, "tiles", up_pairs)
    dn1 = lax.ppermute(dn1, "tiles", dn_pairs)
    up2, dn2 = pack(spectral, sea_mask, G1, G2, False)
    up2 = lax.ppermute(up2, "tiles", up_pairs)
    dn2 = lax.ppermute(dn2, "tiles", dn_pairs)

    freq_pos = (lax.axis_index("bins") * NF + jnp.arange(NF)).astype(F32)
    speed_ratio = jnp.power(1.1, -freq_pos)
    freq_weight = jnp.power(1.03, freq_pos - (NFREQ - 1))
    angles = (jnp.arange(NDIR).astype(F32) + 0.5) * (2.0 * math.pi / NDIR)
    cos_dir = jnp.cos(angles)
    sin_dir = jnp.sin(angles)
    courant = (COURANT_MAX * speed_ratio)[:, None]
    table = jnp.concatenate(
        [
            (courant * jnp.abs(cos_dir)).reshape(-1),
            (courant * jnp.abs(sin_dir)).reshape(-1),
            cos_dir,
            sin_dir,
            freq_weight,
        ]
    )
    sub = jnp.arange(ROWS)
    rows = jnp.stack(
        [sub, jnp.where(sub < 4, sub, sub - ROWS), jnp.where(sub < 4, sub + ROWS, sub)]
    )
    metric = row_metric(first_row + rows, ROWS * count)
    metric = jnp.broadcast_to(metric[:, :, None], (3, ROWS, LANES))

    sea = sea_mask.astype(F32)
    mask = as_tiles(with_wrap(sea))
    strength = 0.5 * friction**2
    wind = jnp.stack(
        [
            strength * jnp.cos(wind_dir),
            strength * jnp.sin(wind_dir),
            1.0 - 0.5 * ice_mask.astype(F32),
        ]
    )
    wind = jnp.pad(wind, ((0, 0), (0, 0), (0, TILES * LANES - NLON)))
    wind = wind.reshape(3, ROWS, TILES, LANES).transpose(0, 2, 1, 3)
    order = jnp.argsort(ocean_owner[0], stable=True).astype(jnp.int32)

    own = own_rows(spectral, table, metric, mask)

    south = jnp.concatenate([sea[:4], edge_mask(up1)], axis=0)
    north = jnp.concatenate([edge_mask(dn1), sea[4:]], axis=0)
    masks = jnp.stack([as_tiles(with_wrap(south)), as_tiles(with_wrap(north))])

    out, acc = finish(table, metric, masks, wind, own, up1, dn1, None, None, 0)
    out, acc = finish(table, metric, masks, wind, own, up2, dn2, acc, out, G1)

    sent = pick_slots(order, acc)
    got = lax.all_to_all(sent, "bins", 0, 0, tiled=True)
    total = got.sum(0)
    rest = total[4:].reshape(2, ROWS, 2, LANES // 2).transpose(0, 2, 1, 3)
    rest = rest.reshape(4, ROWS, LANES // 2)[:, :, : 2 * BLK - LANES]
    fields = jnp.concatenate([total[:4], rest], axis=2).reshape(4, ROWS, 2, BLK)
    return out.reshape(spectrum.shape), fields[:2], fields[2:]


def solution(mesh):
    field = P("tiles", None)
    blocks = P(None, "tiles", "bins", None)
    whole = P("bins", "tiles", None)
    return jax.shard_map(
        shards,
        mesh=mesh,
        in_specs=(whole, field, field, field, field, field),
        out_specs=(whole, blocks, blocks),
        check_vma=False,
    )
```

```python
import math

import jax
import jax.numpy as jnp
from jax import lax
from jax.experimental import pallas as pl
from jax.experimental.pallas import tpu as pltpu
from jax.sharding import PartitionSpec as P

NDIR = 36
NFREQ = 32
LON_BLOCKS = 16
STEPS = 4
COURANT_MAX = 0.6
GRID_STEP = 0.25 * math.pi / 180.0

ROWS = 8
NLON = 1440
BLK = 90
LANES = 128
TILES = 12
TAIL = NLON - (TILES - 1) * LANES
NF = 4
GROUPS = 9
G1 = 6
G2 = GROUPS - G1
TPG = NF * (TILES - 1) + 1

F32 = jnp.float32
PER_STEP = 2
LIMIT = 16 << 20
OFF_BX = 0
OFF_BY = NF * NDIR
OFF_COS = 2 * NF * NDIR
OFF_SIN = OFF_COS + NDIR
OFF_P = OFF_SIN + NDIR


def lane_iota():
    return lax.broadcasted_iota(jnp.int32, (ROWS, LANES), 1)


def sub_iota():
    return lax.broadcasted_iota(jnp.int32, (ROWS, LANES), 0)


def pack_group(src_ref, local, mask_ref, out_ref, group, upward, lane, low):
    def pair(j, i):
        cols = pl.ds(i * LANES, LANES)
        mask = mask_ref[:, cols].astype(F32)
        first = src_ref[j, 2 * local, :, cols] * mask
        second = src_ref[j, 2 * local + 1, :, cols] * mask
        if upward:
            return jnp.where(low, pltpu.roll(first, 4, 0), second)
        return jnp.where(low, first, pltpu.roll(second, 4, 0))

    for i in range(TILES - 1):
        for j in range(NF):
            out_ref[group, j * (TILES - 1) + i] = pair(j, i)
    tail = pair(0, TILES - 1)
    for j in range(1, NF):
        moved = pltpu.roll(pair(j, TILES - 1), TAIL * j, 1)
        tail = jnp.where(lane >= TAIL * j, moved, tail)
    out_ref[group, TPG - 1] = tail


def pack_kernel(width, with_mask, south_ref, north_ref, mask_ref, up_ref, dn_ref):
    lane = lane_iota()
    low = sub_iota() < 4
    for u in range(width):
        g = pl.program_id(0) * width + u
        pack_group(south_ref, u, mask_ref, up_ref, g, True, lane, low)
        pack_group(north_ref, width - 1 - u, mask_ref, dn_ref, g, False, lane, low)
        if with_mask:
            start = jnp.minimum(g, TILES // 2 - 1) * (2 * LANES)
            start = pl.multiple_of(start, 2 * LANES)
            first = mask_ref[:, pl.ds(start, LANES)].astype(F32)
            second = mask_ref[:, pl.ds(start + LANES, LANES)].astype(F32)
            up_ref[g, TPG] = jnp.where(low, pltpu.roll(first, 4, 0), second)
            dn_ref[g, TPG] = jnp.where(low, first, pltpu.roll(second, 4, 0))


def pack(spectral, sea_mask, base, groups, width, with_mask):
    tiles = TPG + 1 if with_mask else TPG
    block = (NF, 2 * width, ROWS, TILES * LANES)
    last = (2 * GROUPS - base) // width - 1
    whole = pl.BlockSpec(memory_space=pltpu.VMEM)
    out = pltpu.VMEM((groups, tiles, ROWS, LANES), F32)
    return pl.pallas_call(
        lambda *refs: pack_kernel(width, with_mask, *refs),
        grid=(groups // width,),
        in_specs=[
            pl.BlockSpec(block, lambda g: (0, base // width + g, 0, 0)),
            pl.BlockSpec(block, lambda g: (0, last - g, 0, 0)),
            pl.BlockSpec((ROWS, TILES * LANES), lambda g: (0, 0)),
        ],
        out_specs=[whole, whole],
        out_shape=[out, out],
        compiler_params=pltpu.CompilerParams(vmem_limit_bytes=LIMIT),
        name="pack%d" % base,
    )(spectral, spectral, sea_mask)


WEST, EAST, BOTH = 0, 1, 2


def fill_wrap(tiles, lane):
    last = tiles[-1]
    after = pltpu.roll(tiles[0], TAIL, 1)
    before = pltpu.roll(last, LANES - TAIL, 1)
    filled = jnp.where(lane < LANES - TAIL, after, before)
    return tiles[:-1] + [jnp.where(lane < TAIL, last, filled)]


def shift_lanes(tiles, west, lane):
    if west:
        moved = [pltpu.roll(t, 1, 1) for t in tiles]
        return [jnp.where(lane == 0, moved[i - 1], moved[i]) for i in range(TILES)]
    moved = [pltpu.roll(t, LANES - 1, 1) for t in tiles]
    return [
        jnp.where(lane == LANES - 1, moved[(i + 1) % TILES], moved[i])
        for i in range(TILES)
    ]


def x_side(direction):
    west = direction < NDIR // 4 or direction >= NDIR - NDIR // 4
    return WEST if west else EAST


def pair_side(dp):
    first, second = x_side(2 * dp), x_side(2 * dp + 1)
    return first if first == second else BOTH


def run_cases(index, values, south_below, side_of, body):
    found = {}
    for v in values:
        found.setdefault((v < south_below, side_of(v)), []).append(v)
    for (south, side), members in sorted(found.items()):
        cond = index == members[0]
        for m in members[1:]:
            cond = jnp.logical_or(cond, index == m)
        pl.when(cond)(lambda south=south, side=side: body(south, side))


def chunk_dps(base, groups):
    south = [base + g for g in range(groups)]
    return south + [2 * GROUPS - 1 - d for d in reversed(south)]


def block_at(base, groups, width, step):
    first = base // width
    if base + groups == GROUPS:
        return first + step
    skip = 2 * (GROUPS - base - groups) // width
    return jnp.where(step < groups // width, first + step, first + skip + step)


def load_tiles(ref):
    return [ref[:, pl.ds(i * LANES, LANES)].astype(F32) for i in range(TILES)]


def own_kernel(
    tab_ref,
    met_ref,
    sea_ref,
    ice_ref,
    friction_ref,
    wind_ref,
    src_ref,
    out_ref,
    mask_ref,
    force_ref,
):
    step = pl.program_id(0)
    lane = lane_iota()
    sub = sub_iota()

    @pl.when(step == 0)
    def _():
        sea = fill_wrap(load_tiles(sea_ref), lane)
        ice = load_tiles(ice_ref)
        friction = load_tiles(friction_ref)
        wind = load_tiles(wind_ref)
        for i in range(TILES):
            strength = 0.5 * friction[i] * friction[i]
            mask_ref[i] = sea[i]
            force_ref[0, i] = strength * jnp.cos(wind[i])
            force_ref[1, i] = strength * jnp.sin(wind[i])
            force_ref[2, i] = 1.0 - 0.5 * ice[i]

    def one(local, carry):
        direction = 2 * PER_STEP * step + local

        def body(south, side):
            west = side == WEST
            inflow = sub > 0 if south else sub < ROWS - 1
            fields = []
            coefs = []
            for j in range(NF):
                cy = tab_ref[OFF_BY + j * NDIR + direction]
                cx = tab_ref[OFF_BX + j * NDIR + direction] * met_ref[0]
                alpha = 1.0 - cx - cy
                coefs.append((alpha, cx, jnp.where(inflow, cy, 0.0)))
                tiles = [
                    src_ref[j, local, :, pl.ds(i * LANES, LANES)] for i in range(TILES)
                ]
                tiles = fill_wrap(tiles, lane)
                fields.append([t * mask_ref[i] for i, t in enumerate(tiles)])
            for sub_step in range(STEPS):
                new = []
                for tiles, (alpha, cx, cy) in zip(fields, coefs):
                    xs = shift_lanes(tiles, west, lane)
                    done = []
                    for i in range(TILES):
                        y = pltpu.roll(tiles[i], 1 if south else ROWS - 1, 0)
                        total = alpha * tiles[i] + cx * xs[i] + cy * y
                        done.append(total * mask_ref[i])
                    new.append(done)
                fields = new
            for j in range(NF):
                for i in range(TILES):
                    out_ref[local // 2, local % 2, j, i] = fields[j][i]

        run_cases(direction, range(NDIR), NDIR // 2, x_side, body)
        return carry

    lax.fori_loop(0, 2 * PER_STEP, one, 0)


def own_rows(spectral, table, metric, sea_mask, ice_mask, friction, wind_dir):
    whole = pl.BlockSpec(memory_space=pltpu.VMEM)
    field = pl.BlockSpec((ROWS, TILES * LANES), lambda i: (0, 0))
    return pl.pallas_call(
        own_kernel,
        grid=(2 * GROUPS // PER_STEP,),
        in_specs=[
            pl.BlockSpec(memory_space=pltpu.SMEM),
            whole,
            field,
            field,
            field,
            field,
            pl.BlockSpec(
                (NF, 2 * PER_STEP, ROWS, TILES * LANES), lambda i: (0, i, 0, 0)
            ),
        ],
        out_specs=[
            pl.BlockSpec(
                (PER_STEP, 2, NF, TILES, ROWS, LANES), lambda i: (i, 0, 0, 0, 0, 0)
            ),
            whole,
            whole,
        ],
        out_shape=[
            jax.ShapeDtypeStruct((2 * GROUPS, 2, NF, TILES, ROWS, LANES), F32),
            pltpu.VMEM((TILES, ROWS, LANES), F32),
            pltpu.VMEM((3, TILES, ROWS, LANES), F32),
        ],
        compiler_params=pltpu.CompilerParams(vmem_limit_bytes=LIMIT),
        name="own",
    )(table, metric, sea_mask, ice_mask, friction, wind_dir, spectral)


def window_masks(mask_ref, up_ref, dn_ref, out_ref, lane, low):
    for side, halo_ref in enumerate((up_ref, dn_ref)):
        rows = []
        for i in range(TILES):
            edge = halo_ref[i // 2, 0]
            if i % 2 != side:
                edge = pltpu.roll(edge, 4, 0)
            mine = pltpu.roll(mask_ref[i], 4, 0)
            if side == 0:
                rows.append(jnp.where(low, edge, mine))
            else:
                rows.append(jnp.where(low, mine, edge))
        rows = fill_wrap(rows, lane)
        for k in range(1, STEPS + 1):
            first = k if side == 0 else 4 - k
            for i in range(TILES):
                window = rows[i]
                if first > 0:
                    window = pltpu.roll(window, ROWS - first, 0)
                out_ref[side, k - 1, i] = jnp.where(
                    low, window, pltpu.roll(window, 4, 0)
                )


def finish_kernel(
    base,
    groups,
    width,
    tab_ref,
    met_ref,
    mask_ref,
    wind_ref,
    own_ref,
    up_ref,
    dn_ref,
    up_mask_ref,
    dn_mask_ref,
    prev_ref,
    old_ref,
    out_ref,
    acc_ref,
    win_ref,
    c_ref,
):
    step = pl.program_id(0)
    dps = chunk_dps(base, groups)
    lane = lane_iota()
    sub = sub_iota()
    low = sub < 4

    @pl.when(step == 0)
    def _():
        if prev_ref is None:
            acc_ref[...] = jnp.zeros_like(acc_ref)
            window_masks(mask_ref, up_mask_ref, dn_mask_ref, win_ref, lane, low)
        else:
            acc_ref[...] = prev_ref[...]

    windows = win_ref if prev_ref is None else mask_ref

    def one(local, carry):
        dp = block_at(base, groups, width, step) * width + local

        def contribution(south, side):
            halo_ref = up_ref if south else dn_ref
            row = 0 if south else 1
            group = local if south else width - 1 - local
            fields = []
            scalars = []
            for j in range(NF):
                index = j * NDIR + 2 * dp
                bx = jnp.where(low, tab_ref[OFF_BX + index], tab_ref[OFF_BX + index + 1])
                cy = jnp.where(low, tab_ref[OFF_BY + index], tab_ref[OFF_BY + index + 1])
                inside = sub % 4 < 3 if south else sub % 4 > 0
                scalars.append((bx, cy, jnp.where(inside, 1.0 - cy, 0.0)))
                tiles = [halo_ref[group, j * (TILES - 1) + i] for i in range(TILES - 1)]
                last = halo_ref[group, TPG - 1]
                if j > 0:
                    last = pltpu.roll(last, LANES - TAIL * j, 1)
                fields.append(fill_wrap(tiles + [last], lane))
            for k in range(STEPS):
                new = []
                for tiles, (bx, cy, rest) in zip(fields, scalars):
                    cx = bx * met_ref[1 + row * STEPS + k]
                    alpha = rest - cx
                    ahead = [pltpu.roll(t, ROWS - 1 if south else 1, 0) for t in tiles]
                    if side == BOTH:
                        west = shift_lanes(ahead, True, lane)
                        east = shift_lanes(ahead, False, lane)
                        here = low if south else jnp.logical_not(low)
                        xs = [jnp.where(here, w, e) for w, e in zip(west, east)]
                    else:
                        xs = shift_lanes(ahead, side == WEST, lane)
                    new.append(
                        [
                            (alpha * ahead[i] + cx * xs[i] + cy * tiles[i])
                            * windows[row, k, i]
                            for i in range(TILES)
                        ]
                    )
                fields = new
            for j in range(NF):
                for i in range(TILES):
                    c_ref[j, i] = fields[j][i]

        run_cases(dp, dps, GROUPS, pair_side, contribution)

        def combine(south, side):
            weight = [tab_ref[OFF_P + j] for j in range(NF)]
            angle = [
                (tab_ref[OFF_COS + 2 * dp + dd], tab_ref[OFF_SIN + 2 * dp + dd])
                for dd in range(2)
            ]
            target = low if south else jnp.logical_not(low)
            for i in range(TILES):
                ice = wind_ref[2, i]
                parts = []
                for j in range(NF):
                    c = c_ref[j, i]
                    turned = pltpu.roll(c, 4, 0)
                    parts.append((c, turned) if south else (turned, c))
                total = [acc_ref[n, i] for n in range(4)]
                for dd in range(2):
                    cos_d, sin_d = angle[dd]
                    h = cos_d * wind_ref[0, i] + sin_d * wind_ref[1, i]
                    h = jnp.maximum(h, 0.0)
                    for j in range(NF):
                        e = own_ref[local, dd, j, i] + jnp.where(target, parts[j][dd], 0.0)
                        x = weight[j] * e
                        out_ref[j, 2 * local + dd, :, pl.ds(i * LANES, LANES)] = (e + h * x) * ice
                        y = weight[j] * x
                        sum_x = x if j == 0 else sum_x + x
                        sum_y = y if j == 0 else sum_y + y
                    source = h * sum_x
                    drift = ice * (sum_x + h * sum_y)
                    total[0] += cos_d * drift
                    total[1] += sin_d * drift
                    total[2] += cos_d * source
                    total[3] += sin_d * source
                for n in range(4):
                    acc_ref[n, i] = total[n]

        run_cases(dp, dps, GROUPS, lambda d: WEST, combine)
        return carry

    lax.fori_loop(0, width, one, 0)


def in_vmem(x):
    return pltpu.with_memory_space_constraint(x, pltpu.VMEM)


def in_hbm(x):
    return pltpu.with_memory_space_constraint(x, pltpu.HBM)


def finish(table, metric, mask, wind, own, up, dn, prev, old, base, width):
    groups = up.shape[0]
    tiles = up.shape[1]
    steps = groups // width
    whole = pl.BlockSpec(memory_space=pltpu.VMEM)
    acc = pltpu.VMEM((4, TILES, ROWS, LANES), F32)
    out = jax.ShapeDtypeStruct((NF, NDIR, ROWS, NLON), F32)
    halo = (width, tiles, ROWS, LANES)
    block = lambda i: block_at(base, groups, width, i)
    in_specs = [
        pl.BlockSpec(memory_space=pltpu.SMEM),
        whole,
        whole,
        whole,
        pl.BlockSpec(
            (width, 2, NF, TILES, ROWS, LANES), lambda i: (block(i), 0, 0, 0, 0, 0)
        ),
        pl.BlockSpec(halo, lambda i: (jnp.minimum(i, steps - 1), 0, 0, 0)),
        pl.BlockSpec(
            halo, lambda i: (jnp.minimum(2 * steps - 1 - i, steps - 1), 0, 0, 0)
        ),
    ]
    args = [table, metric, in_vmem(mask), in_vmem(wind), own, in_hbm(up), in_hbm(dn)]
    out_specs = [
        pl.BlockSpec(
            (NF, 2 * width, ROWS, TILES * LANES), lambda i: (0, block(i), 0, 0)
        ),
        whole,
    ]
    out_shape = [out, acc]
    aliases = {}
    setting = (base, groups, width)
    if prev is None:
        kernel = lambda *r: finish_kernel(*setting, *r[:9], None, None, *r[9:])
        edges = pl.BlockSpec((TILES // 2, 1, ROWS, LANES), lambda i: (0, TPG, 0, 0))
        in_specs += [edges, edges]
        args += args[5:7]
        out_specs.append(whole)
        out_shape.append(pltpu.VMEM((2, STEPS, TILES, ROWS, LANES), F32))
    else:
        kernel = lambda *r: finish_kernel(
            *setting, *r[:7], None, None, *r[7:11], None, *r[11:]
        )
        in_specs += [whole, pl.BlockSpec(memory_space=pl.ANY)]
        args += [in_vmem(prev), old]
        aliases = {8: 0}
    return pl.pallas_call(
        kernel,
        grid=(2 * steps,),
        in_specs=in_specs,
        out_specs=out_specs,
        out_shape=out_shape,
        scratch_shapes=[pltpu.VMEM((NF, TILES, ROWS, LANES), F32)],
        input_output_aliases=aliases,
        compiler_params=pltpu.CompilerParams(vmem_limit_bytes=LIMIT),
        name="finish%d" % base,
    )(*args)


def slots_kernel(owner_ref, acc_ref, out_ref, order_ref, count_ref):
    lane = lane_iota()
    for k in range(LON_BLOCKS // 2):
        count_ref[k] = 0
    for block in range(LON_BLOCKS):
        owner = owner_ref[0, block]
        seen = count_ref[owner]
        order_ref[2 * owner + seen] = block
        count_ref[owner] = seen + 1

    for k in range(LON_BLOCKS // 2):
        rests = []
        for c in range(4):
            parts = []
            for s in range(2):
                column = order_ref[2 * k + s] * BLK
                tile = column // LANES
                shift = column % LANES
                back = (LANES - shift) % LANES
                here = pltpu.roll(acc_ref[c, tile], back, 1)
                after = pltpu.roll(acc_ref[c, jnp.minimum(tile + 1, TILES - 1)], back, 1)
                parts.append(jnp.where(lane < LANES - shift, here, after))
            moved = pltpu.roll(parts[1], BLK, 1)
            out_ref[k, c] = jnp.where(lane < BLK, parts[0], moved)
            rests.append(moved)
        for c in range(2):
            other = pltpu.roll(rests[2 * c + 1], LANES // 2, 1)
            both = jnp.where(lane < LANES // 2, rests[2 * c], other)
            used = lane % (LANES // 2) < 2 * BLK - LANES
            out_ref[k, 4 + c] = jnp.where(used, both, 0.0)


def pick_slots(owner, acc):
    return pl.pallas_call(
        slots_kernel,
        in_specs=[
            pl.BlockSpec(memory_space=pltpu.SMEM),
            pl.BlockSpec(memory_space=pltpu.VMEM),
        ],
        out_specs=pl.BlockSpec(memory_space=pltpu.VMEM),
        out_shape=pltpu.VMEM((LON_BLOCKS // 2, 6, ROWS, LANES), F32),
        scratch_shapes=[
            pltpu.SMEM((LON_BLOCKS,), jnp.int32),
            pltpu.SMEM((LON_BLOCKS // 2,), jnp.int32),
        ],
        compiler_params=pltpu.CompilerParams(vmem_limit_bytes=LIMIT),
        name="slots",
    )(owner, acc)


def row_metric(row_pos, lat_total):
    latitude = (row_pos.astype(F32) - lat_total / 2 + 0.5) * GRID_STEP
    edge_lat = (lat_total / 2 - 0.5) * GRID_STEP
    return jnp.cos(jnp.asarray(edge_lat, F32)) / jnp.cos(latitude)


def shards(spectrum, sea_mask, ice_mask, friction, wind_dir, ocean_owner):
    count = lax.axis_size("tiles")
    first_row = lax.axis_index("tiles") * ROWS
    up_pairs = [(i, i + 1) for i in range(count - 1)]
    dn_pairs = [(i + 1, i) for i in range(count - 1)]
    spectral = spectrum.reshape(NF, NDIR, ROWS, NLON)
    spectral = pltpu.with_memory_space_constraint(spectral, pltpu.HBM)

    up1, dn1 = pack(spectral, sea_mask, 0, G1, 2, True)
    sea_later, _, _ = lax.optimization_barrier((sea_mask, up1, dn1))
    up1 = lax.ppermute(up1, "tiles", up_pairs)
    dn1 = lax.ppermute(dn1, "tiles", dn_pairs)
    up2, dn2 = pack(spectral, sea_later, G1, G2, G2, False)
    up2 = lax.ppermute(up2, "tiles", up_pairs)
    dn2 = lax.ppermute(dn2, "tiles", dn_pairs)

    freq_pos = (lax.axis_index("bins") * NF + jnp.arange(NF)).astype(F32)
    speed_ratio = jnp.power(1.1, -freq_pos)
    freq_weight = jnp.power(1.03, freq_pos - (NFREQ - 1))
    angles = (jnp.arange(NDIR).astype(F32) + 0.5) * (2.0 * math.pi / NDIR)
    cos_dir = jnp.cos(angles)
    sin_dir = jnp.sin(angles)
    courant = (COURANT_MAX * speed_ratio)[:, None]
    table = jnp.concatenate(
        [
            (courant * jnp.abs(cos_dir)).reshape(-1),
            (courant * jnp.abs(sin_dir)).reshape(-1),
            cos_dir,
            sin_dir,
            freq_weight,
        ]
    )
    sub = jnp.arange(ROWS)
    part = sub % 4
    rows = [sub]
    keep = [jnp.ones_like(sub)]
    for k in range(1, STEPS + 1):
        rows.append(part - 4 + k)
        keep.append(part < 3)
    for k in range(1, STEPS + 1):
        rows.append(part + ROWS - k)
        keep.append(part > 0)
    metric = row_metric(first_row + jnp.stack(rows), ROWS * count)
    metric = metric * jnp.stack(keep).astype(F32)
    metric = jnp.broadcast_to(metric[:, :, None], (1 + 2 * STEPS, ROWS, LANES))

    own, mask, wind = own_rows(
        spectral, table, metric, sea_mask, ice_mask, friction, wind_dir
    )
    out, acc, windows = finish(
        table, metric, mask, wind, own, up1, dn1, None, None, 0, PER_STEP
    )
    out, acc = finish(table, metric, windows, wind, own, up2, dn2, acc, out, G1, 1)

    sent = pick_slots(ocean_owner, acc)
    got = lax.all_to_all(sent, "bins", 0, 0, tiled=True)
    total = got.sum(0)
    rest = total[4:].reshape(2, ROWS, 2, LANES // 2).transpose(0, 2, 1, 3)
    rest = rest.reshape(4, ROWS, LANES // 2)[:, :, : 2 * BLK - LANES]
    fields = jnp.concatenate([total[:4], rest], axis=2).reshape(4, ROWS, 2, BLK)
    return out.reshape(spectrum.shape), fields[:2], fields[2:]


def solution(mesh):
    field = P("tiles", None)
    blocks = P(None, "tiles", "bins", None)
    whole = P("bins", "tiles", None)
    return jax.shard_map(
        shards,
        mesh=mesh,
        in_specs=(whole, field, field, field, field, field),
        out_specs=(whole, blocks, blocks),
        check_vma=False,
    )
```

```python
import math

import jax
import jax.numpy as jnp
import numpy as np
from jax import lax
from jax.experimental import pallas as pl
from jax.experimental.pallas import tpu as pltpu
from jax.sharding import PartitionSpec as P

NDIR = 36
NFREQ = 32
LON_BLOCKS = 16
STEPS = 4
COURANT_MAX = 0.6
GRID_STEP = 0.25 * math.pi / 180.0

ROWS = 8
NLON = 1440
BLK = 90
LANES = 128
TILES = 12
TAIL = NLON - (TILES - 1) * LANES
NF = 4
GROUPS = 9
G1 = 6
G2 = GROUPS - G1
TPG = NF * (TILES - 1) + 1

F32 = jnp.float32
PER_STEP = 2
LIMIT = 16 << 20
ANGLES = (np.arange(NDIR, dtype=np.float32) + 0.5) * np.float32(2.0 * math.pi / NDIR)
TRIG = np.concatenate([np.cos(ANGLES), np.sin(ANGLES)]).astype(np.float32)


def lane_iota():
    return lax.broadcasted_iota(jnp.int32, (ROWS, LANES), 1)


def sub_iota():
    return lax.broadcasted_iota(jnp.int32, (ROWS, LANES), 0)


def pack_group(src_ref, local, mask_ref, out_ref, group, upward, lane, low):
    def pair(j, i):
        cols = pl.ds(i * LANES, LANES)
        mask = mask_ref[:, cols].astype(F32)
        first = src_ref[j, 2 * local, :, cols] * mask
        second = src_ref[j, 2 * local + 1, :, cols] * mask
        if upward:
            return jnp.where(low, pltpu.roll(first, 4, 0), second)
        return jnp.where(low, first, pltpu.roll(second, 4, 0))

    for i in range(TILES - 1):
        for j in range(NF):
            out_ref[group, j * (TILES - 1) + i] = pair(j, i)
    tail = pair(0, TILES - 1)
    for j in range(1, NF):
        moved = pltpu.roll(pair(j, TILES - 1), TAIL * j, 1)
        tail = jnp.where(lane >= TAIL * j, moved, tail)
    out_ref[group, TPG - 1] = tail


def pack_kernel(base, width, with_mask, up_ref, src_ref, mask_ref, out_ref):
    lane = lane_iota()
    low = sub_iota() < 4
    upward = up_ref[0] == 1

    def fill(is_up):
        for u in range(width):
            g = pl.program_id(0) * width + u
            local = u if is_up else width - 1 - u
            pack_group(src_ref, local, mask_ref, out_ref, g, is_up, lane, low)
            if with_mask:
                start = jnp.minimum(g, TILES // 2 - 1) * (2 * LANES)
                start = pl.multiple_of(start, 2 * LANES)
                first = mask_ref[:, pl.ds(start, LANES)].astype(F32)
                second = mask_ref[:, pl.ds(start + LANES, LANES)].astype(F32)
                if is_up:
                    first = pltpu.roll(first, 4, 0)
                else:
                    second = pltpu.roll(second, 4, 0)
                out_ref[g, TPG] = jnp.where(low, first, second)

    pl.when(upward)(lambda: fill(True))
    pl.when(jnp.logical_not(upward))(lambda: fill(False))


def block_of(base, width, step, south):
    last = (2 * GROUPS - base) // width - 1
    return jnp.where(south == 1, base // width + step, last - step)


def pack(upward, spectral, sea_mask, base, groups, width, with_mask, name):
    tiles = TPG + 1 if with_mask else TPG
    block = (NF, 2 * width, ROWS, TILES * LANES)
    return pl.pallas_call(
        lambda *refs: pack_kernel(base, width, with_mask, *refs),
        grid_spec=pltpu.PrefetchScalarGridSpec(
            num_scalar_prefetch=1,
            grid=(groups // width,),
            in_specs=[
                pl.BlockSpec(
                    block, lambda g, up: (0, block_of(base, width, g, up[0]), 0, 0)
                ),
                pl.BlockSpec((ROWS, TILES * LANES), lambda g, up: (0, 0)),
            ],
            out_specs=pl.BlockSpec(memory_space=pltpu.VMEM),
        ),
        out_shape=pltpu.VMEM((groups, tiles, ROWS, LANES), F32),
        compiler_params=pltpu.CompilerParams(vmem_limit_bytes=LIMIT),
        name=name,
    )(upward, spectral, sea_mask)


WEST, EAST, BOTH = 0, 1, 2


def fill_wrap(tiles, lane):
    last = tiles[-1]
    after = pltpu.roll(tiles[0], TAIL, 1)
    before = pltpu.roll(last, LANES - TAIL, 1)
    filled = jnp.where(lane < LANES - TAIL, after, before)
    return tiles[:-1] + [jnp.where(lane < TAIL, last, filled)]


def shift_lanes(tiles, west, lane):
    if west:
        moved = [pltpu.roll(t, 1, 1) for t in tiles]
        return [jnp.where(lane == 0, moved[i - 1], moved[i]) for i in range(TILES)]
    moved = [pltpu.roll(t, LANES - 1, 1) for t in tiles]
    return [
        jnp.where(lane == LANES - 1, moved[(i + 1) % TILES], moved[i])
        for i in range(TILES)
    ]


def x_side(direction):
    west = direction < NDIR // 4 or direction >= NDIR - NDIR // 4
    return WEST if west else EAST


def pair_side(dp):
    first, second = x_side(2 * dp), x_side(2 * dp + 1)
    return first if first == second else BOTH


def run_cases(index, values, south_below, side_of, body):
    found = {}
    for v in values:
        found.setdefault((v < south_below, side_of(v)), []).append(v)
    for (south, side), members in sorted(found.items()):
        cond = index == members[0]
        for m in members[1:]:
            cond = jnp.logical_or(cond, index == m)
        pl.when(cond)(lambda south=south, side=side: body(south, side))


def load_tiles(ref):
    return [ref[:, pl.ds(i * LANES, LANES)].astype(F32) for i in range(TILES)]


def fill_metric(first_row, lat_total, out_ref):
    sub = sub_iota()
    part = sub % 4
    rows = [(sub, sub >= 0)]
    rows += [(part - 4 + k, part < 3) for k in range(1, STEPS + 1)]
    rows += [(part + ROWS - k, part > 0) for k in range(1, STEPS + 1)]
    edge = math.cos((lat_total / 2 - 0.5) * GRID_STEP)
    for n, (row, inside) in enumerate(rows):
        row = (first_row + row).astype(F32)
        latitude = (row - lat_total / 2 + 0.5) * GRID_STEP
        out_ref[n] = jnp.where(inside, edge / jnp.cos(latitude), 0.0)


def own_kernel(
    lat_total,
    tab_ref,
    trig_ref,
    row_ref,
    sea_ref,
    ice_ref,
    friction_ref,
    wind_ref,
    src_ref,
    out_ref,
    mask_ref,
    force_ref,
    met_ref,
):
    step = pl.program_id(0)
    lane = lane_iota()
    sub = sub_iota()

    @pl.when(step == 0)
    def _():
        sea = fill_wrap(load_tiles(sea_ref), lane)
        ice = load_tiles(ice_ref)
        friction = load_tiles(friction_ref)
        wind = load_tiles(wind_ref)
        for i in range(TILES):
            strength = 0.5 * friction[i] * friction[i]
            mask_ref[i] = sea[i]
            force_ref[0, i] = strength * jnp.cos(wind[i])
            force_ref[1, i] = strength * jnp.sin(wind[i])
            force_ref[2, i] = 1.0 - 0.5 * ice[i]
        fill_metric(row_ref[0], lat_total, met_ref)

    def one(local, carry):
        direction = 2 * PER_STEP * step + local

        def body(south, side):
            west = side == WEST
            inflow = sub > 0 if south else sub < ROWS - 1
            fields = []
            coefs = []
            for j in range(NF):
                cy = tab_ref[j] * jnp.abs(trig_ref[NDIR + direction])
                cx = tab_ref[j] * jnp.abs(trig_ref[direction]) * met_ref[0]
                alpha = 1.0 - cx - cy
                coefs.append((alpha, cx, jnp.where(inflow, cy, 0.0)))
                tiles = [
                    src_ref[j, local, :, pl.ds(i * LANES, LANES)] for i in range(TILES)
                ]
                tiles = fill_wrap(tiles, lane)
                fields.append([t * mask_ref[i] for i, t in enumerate(tiles)])
            for sub_step in range(STEPS):
                new = []
                for tiles, (alpha, cx, cy) in zip(fields, coefs):
                    xs = shift_lanes(tiles, west, lane)
                    done = []
                    for i in range(TILES):
                        y = pltpu.roll(tiles[i], 1 if south else ROWS - 1, 0)
                        total = alpha * tiles[i] + cx * xs[i] + cy * y
                        done.append(total * mask_ref[i])
                    new.append(done)
                fields = new
            for j in range(NF):
                for i in range(TILES):
                    out_ref[local // 2, local % 2, j, i] = fields[j][i]

        run_cases(direction, range(NDIR), NDIR // 2, x_side, body)
        return carry

    lax.fori_loop(0, 2 * PER_STEP, one, 0)


def own_rows(
    spectral, table, trig, first_row, lat_total, sea_mask, ice_mask, friction, wind_dir
):
    whole = pl.BlockSpec(memory_space=pltpu.VMEM)
    field = pl.BlockSpec((ROWS, TILES * LANES), lambda i: (0, 0))
    return pl.pallas_call(
        lambda *refs: own_kernel(lat_total, *refs),
        grid=(2 * GROUPS // PER_STEP,),
        in_specs=[
            pl.BlockSpec(memory_space=pltpu.SMEM),
            pl.BlockSpec(memory_space=pltpu.SMEM),
            pl.BlockSpec(memory_space=pltpu.SMEM),
            field,
            field,
            field,
            field,
            pl.BlockSpec(
                (NF, 2 * PER_STEP, ROWS, TILES * LANES), lambda i: (0, i, 0, 0)
            ),
        ],
        out_specs=[
            pl.BlockSpec(
                (PER_STEP, 2, NF, TILES, ROWS, LANES), lambda i: (i, 0, 0, 0, 0, 0)
            ),
            whole,
            whole,
            whole,
        ],
        out_shape=[
            jax.ShapeDtypeStruct((2 * GROUPS, 2, NF, TILES, ROWS, LANES), F32),
            pltpu.VMEM((TILES, ROWS, LANES), F32),
            pltpu.VMEM((3, TILES, ROWS, LANES), F32),
            pltpu.VMEM((1 + 2 * STEPS, ROWS, LANES), F32),
        ],
        compiler_params=pltpu.CompilerParams(vmem_limit_bytes=LIMIT),
        name="own",
    )(table, trig, first_row, sea_mask, ice_mask, friction, wind_dir, spectral)


def window_masks(south, mask_ref, halo_ref, out_ref, lane, low):
    rows = []
    for i in range(TILES):
        edge = halo_ref[i // 2, 0]
        if (i % 2 == 0) != south:
            edge = pltpu.roll(edge, 4, 0)
        mine = pltpu.roll(mask_ref[i], 4, 0)
        if south:
            rows.append(jnp.where(low, edge, mine))
        else:
            rows.append(jnp.where(low, mine, edge))
    rows = fill_wrap(rows, lane)
    for k in range(1, STEPS + 1):
        first = k if south else 4 - k
        for i in range(TILES):
            window = rows[i]
            if first > 0:
                window = pltpu.roll(window, ROWS - first, 0)
            out_ref[k - 1, i] = jnp.where(low, window, pltpu.roll(window, 4, 0))


def finish_kernel(
    base,
    groups,
    width,
    south_ref,
    tab_ref,
    trig_ref,
    met_ref,
    mask_ref,
    wind_ref,
    own_ref,
    halo_ref,
    edge_ref,
    prev_ref,
    old_ref,
    out_ref,
    acc_ref,
    win_ref,
    c_ref,
):
    step = pl.program_id(0)
    is_south = south_ref[0] == 1
    dps = [base + g for g in range(groups)]
    dps = dps + [2 * GROUPS - 1 - d for d in dps]
    lane = lane_iota()
    sub = sub_iota()
    low = sub < 4

    @pl.when(step == 0)
    def _():
        if prev_ref is None:
            acc_ref[...] = jnp.zeros_like(acc_ref)
        else:
            acc_ref[...] = prev_ref[...]

    if edge_ref is not None:
        for south in (True, False):
            mine = jnp.logical_and(step == 0, is_south == south)
            pl.when(mine)(
                lambda south=south: window_masks(
                    south, mask_ref, edge_ref, win_ref, lane, low
                )
            )

    windows = mask_ref if edge_ref is None else win_ref

    def one(u, carry):
        local = jnp.where(is_south, u, width - 1 - u)
        group = base + step * width + u
        dp = jnp.where(is_south, group, 2 * GROUPS - 1 - group)

        def contribution(south, side):
            row = 0 if south else 1
            fields = []
            scalars = []
            for j in range(NF):
                courant = tab_ref[j]
                bx = courant * jnp.abs(
                    jnp.where(low, trig_ref[2 * dp], trig_ref[2 * dp + 1])
                )
                cy = courant * jnp.abs(
                    jnp.where(low, trig_ref[NDIR + 2 * dp], trig_ref[NDIR + 2 * dp + 1])
                )
                inside = sub % 4 < 3 if south else sub % 4 > 0
                scalars.append((bx, cy, jnp.where(inside, 1.0 - cy, 0.0)))
                tiles = [halo_ref[u, j * (TILES - 1) + i] for i in range(TILES - 1)]
                last = halo_ref[u, TPG - 1]
                if j > 0:
                    last = pltpu.roll(last, LANES - TAIL * j, 1)
                fields.append(fill_wrap(tiles + [last], lane))
            for k in range(STEPS):
                new = []
                for tiles, (bx, cy, rest) in zip(fields, scalars):
                    cx = bx * met_ref[1 + row * STEPS + k]
                    alpha = rest - cx
                    ahead = [pltpu.roll(t, ROWS - 1 if south else 1, 0) for t in tiles]
                    if side == BOTH:
                        west = shift_lanes(ahead, True, lane)
                        east = shift_lanes(ahead, False, lane)
                        here = low if south else jnp.logical_not(low)
                        xs = [jnp.where(here, w, e) for w, e in zip(west, east)]
                    else:
                        xs = shift_lanes(ahead, side == WEST, lane)
                    new.append(
                        [
                            (alpha * ahead[i] + cx * xs[i] + cy * tiles[i])
                            * windows[k, i]
                            for i in range(TILES)
                        ]
                    )
                fields = new
            for j in range(NF):
                for i in range(TILES):
                    c_ref[j, i] = fields[j][i]

        run_cases(dp, dps, GROUPS, pair_side, contribution)

        def combine(south, side):
            weight = [tab_ref[NF + j] for j in range(NF)]
            angle = [
                (trig_ref[2 * dp + dd], trig_ref[NDIR + 2 * dp + dd]) for dd in range(2)
            ]
            target = low if south else jnp.logical_not(low)
            for first in range(0, TILES, 2):
                held = []
                for i in (first, first + 1):
                    held.append(
                        (
                            [wind_ref[n, i] for n in range(3)],
                            [c_ref[j, i] for j in range(NF)],
                            [acc_ref[n, i] for n in range(4)],
                            [
                                [own_ref[local, dd, j, i] for j in range(NF)]
                                for dd in range(2)
                            ],
                        )
                    )
                results = []
                for (east, north, ice), parts, total, own in held:
                    made = []
                    for dd in range(2):
                        cos_d, sin_d = angle[dd]
                        h = jnp.maximum(cos_d * east + sin_d * north, 0.0)
                        for j in range(NF):
                            c = parts[j]
                            if (dd == 0) != south:
                                c = pltpu.roll(c, 4, 0)
                            e = own[dd][j] + jnp.where(target, c, 0.0)
                            x = weight[j] * e
                            made.append((e + h * x) * ice)
                            y = weight[j] * x
                            sum_x = x if j == 0 else sum_x + x
                            sum_y = y if j == 0 else sum_y + y
                        source = h * sum_x
                        drift = ice * (sum_x + h * sum_y)
                        total = [
                            total[0] + cos_d * drift,
                            total[1] + sin_d * drift,
                            total[2] + cos_d * source,
                            total[3] + sin_d * source,
                        ]
                    results.append((made, total))
                for i, (made, total) in zip((first, first + 1), results):
                    cols = pl.ds(i * LANES, LANES)
                    for dd in range(2):
                        for j in range(NF):
                            out_ref[j, 2 * local + dd, :, cols] = made[dd * NF + j]
                    for n in range(4):
                        acc_ref[n, i] = total[n]

        run_cases(dp, dps, GROUPS, lambda d: WEST, combine)
        return carry

    lax.fori_loop(0, width, one, 0)


def in_vmem(x):
    return pltpu.with_memory_space_constraint(x, pltpu.VMEM)


def in_hbm(x):
    return pltpu.with_memory_space_constraint(x, pltpu.HBM)


def finish(south, table, trig, metric, mask, wind, own, halo, prev, old, base, width, name):
    groups, tiles = halo.shape[:2]
    whole = pl.BlockSpec(memory_space=pltpu.VMEM)
    block = lambda i, s: block_of(base, width, i, s[0])
    in_specs = [
        pl.BlockSpec(memory_space=pltpu.SMEM),
        pl.BlockSpec(memory_space=pltpu.SMEM),
        whole,
        whole,
        whole,
        pl.BlockSpec(
            (width, 2, NF, TILES, ROWS, LANES),
            lambda i, s: (block(i, s), 0, 0, 0, 0, 0),
        ),
        pl.BlockSpec((width, tiles, ROWS, LANES), lambda i, s: (i, 0, 0, 0)),
    ]
    halo = in_hbm(halo)
    args = [south, table, trig, in_vmem(metric), in_vmem(mask), in_vmem(wind)]
    args += [own, halo]
    out_specs = [
        pl.BlockSpec(
            (NF, 2 * width, ROWS, TILES * LANES), lambda i, s: (0, block(i, s), 0, 0)
        ),
        whole,
    ]
    out_shape = [
        jax.ShapeDtypeStruct((NF, NDIR, ROWS, NLON), F32),
        pltpu.VMEM((4, TILES, ROWS, LANES), F32),
    ]
    with_edge = tiles > TPG
    with_prev = prev is not None
    aliases = {}
    if with_edge:
        in_specs.append(
            pl.BlockSpec((TILES // 2, 1, ROWS, LANES), lambda i, s: (0, TPG, 0, 0))
        )
        args.append(halo)
        out_specs.append(whole)
        out_shape.append(pltpu.VMEM((STEPS, TILES, ROWS, LANES), F32))
    if with_prev:
        in_specs += [whole, pl.BlockSpec(memory_space=pl.ANY)]
        args += [in_vmem(prev), old]
        aliases = {len(args) - 1: 0}

    def kernel(*refs):
        refs = list(refs)
        fixed, refs = refs[:8], refs[8:]
        edge = refs.pop(0) if with_edge else None
        before = refs.pop(0) if with_prev else None
        former = refs.pop(0) if with_prev else None
        result, acc = refs.pop(0), refs.pop(0)
        windows = refs.pop(0) if with_edge else None
        finish_kernel(
            base,
            groups,
            width,
            *fixed,
            edge,
            before,
            former,
            result,
            acc,
            windows,
            *refs,
        )

    return pl.pallas_call(
        kernel,
        grid_spec=pltpu.PrefetchScalarGridSpec(
            num_scalar_prefetch=1,
            grid=(groups // width,),
            in_specs=in_specs,
            out_specs=out_specs,
            scratch_shapes=[pltpu.VMEM((NF, TILES, ROWS, LANES), F32)],
        ),
        out_shape=out_shape,
        input_output_aliases=aliases,
        compiler_params=pltpu.CompilerParams(vmem_limit_bytes=LIMIT),
        name=name,
    )(*args)


def slots_kernel(owner_ref, acc_ref, out_ref, order_ref, count_ref):
    lane = lane_iota()
    for k in range(LON_BLOCKS // 2):
        count_ref[k] = 0
    for block in range(LON_BLOCKS):
        owner = owner_ref[0, block]
        seen = count_ref[owner]
        order_ref[2 * owner + seen] = block
        count_ref[owner] = seen + 1

    for k in range(LON_BLOCKS // 2):
        rests = []
        for c in range(4):
            parts = []
            for s in range(2):
                column = order_ref[2 * k + s] * BLK
                tile = column // LANES
                shift = column % LANES
                back = (LANES - shift) % LANES
                here = pltpu.roll(acc_ref[c, tile], back, 1)
                after = pltpu.roll(acc_ref[c, jnp.minimum(tile + 1, TILES - 1)], back, 1)
                parts.append(jnp.where(lane < LANES - shift, here, after))
            moved = pltpu.roll(parts[1], BLK, 1)
            out_ref[k, c] = jnp.where(lane < BLK, parts[0], moved)
            rests.append(moved)
        for c in range(2):
            other = pltpu.roll(rests[2 * c + 1], LANES // 2, 1)
            both = jnp.where(lane < LANES // 2, rests[2 * c], other)
            used = lane % (LANES // 2) < 2 * BLK - LANES
            out_ref[k, 4 + c] = jnp.where(used, both, 0.0)


def pick_slots(owner, acc):
    return pl.pallas_call(
        slots_kernel,
        in_specs=[
            pl.BlockSpec(memory_space=pltpu.SMEM),
            pl.BlockSpec(memory_space=pltpu.VMEM),
        ],
        out_specs=pl.BlockSpec(memory_space=pltpu.VMEM),
        out_shape=pltpu.VMEM((LON_BLOCKS // 2, 6, ROWS, LANES), F32),
        scratch_shapes=[
            pltpu.SMEM((LON_BLOCKS,), jnp.int32),
            pltpu.SMEM((LON_BLOCKS // 2,), jnp.int32),
        ],
        compiler_params=pltpu.CompilerParams(vmem_limit_bytes=LIMIT),
        name="slots",
    )(owner, acc)


def shards(spectrum, sea_mask, ice_mask, friction, wind_dir, ocean_owner):
    count = lax.axis_size("tiles")
    first_row = (lax.axis_index("tiles") * ROWS).astype(jnp.int32).reshape(1)
    spectral = in_hbm(spectrum.reshape(NF, NDIR, ROWS, NLON))
    sea = in_hbm(sea_mask)
    odd = lax.axis_index("tiles") % 2
    odd = odd.astype(jnp.int32).reshape(1)
    even = 1 - odd

    def swap(x, start):
        pairs = [(i, i + 1) for i in range(start, count - 1, 2)]
        return lax.ppermute(x, "tiles", pairs + [(j, i) for i, j in pairs])

    far1 = pack(odd, spectral, sea, 0, G1, 2, True, "far1")
    sea, _ = lax.optimization_barrier((sea, far1))
    far1 = swap(far1, 1)
    near = pack(even, spectral, sea, 0, GROUPS, 3, True, "near")
    sea, _ = lax.optimization_barrier((sea, near))
    near = swap(near, 0)
    far2 = pack(odd, spectral, sea, G1, G2, G2, False, "far2")
    far2 = swap(far2, 1)

    place = np.tile(np.arange(NF), 2)
    speeds = np.arange(2 * NF) < NF
    freq_pos = (lax.axis_index("bins") * NF + place).astype(F32)
    power = jnp.where(speeds, -freq_pos, freq_pos - (NFREQ - 1))
    table = jnp.power(jnp.where(speeds, 1.1, 1.03).astype(F32), power)
    table = table * jnp.where(speeds, COURANT_MAX, 1.0).astype(F32)
    trig = jnp.asarray(TRIG)

    own, mask, wind, metric = own_rows(
        spectral,
        table,
        trig,
        first_row,
        count * ROWS,
        sea,
        ice_mask,
        friction,
        wind_dir,
    )
    common = (table, trig, metric)
    out, acc, windows = finish(
        even, *common, mask, wind, own, far1, None, None, 0, 2, "finish_far1"
    )
    out, acc, _ = finish(
        odd, *common, mask, wind, own, near, acc, out, 0, 3, "finish_near"
    )
    out, acc = finish(
        even, *common, windows, wind, own, far2, acc, out, G1, 1, "finish_far2"
    )

    sent = pick_slots(ocean_owner, acc)
    got = lax.all_to_all(sent, "bins", 0, 0, tiled=True)
    total = got.sum(0)
    rest = total[4:].reshape(2, ROWS, 2, LANES // 2).transpose(0, 2, 1, 3)
    rest = rest.reshape(4, ROWS, LANES // 2)[:, :, : 2 * BLK - LANES]
    fields = jnp.concatenate([total[:4], rest], axis=2).reshape(4, ROWS, 2, BLK)
    return out.reshape(spectrum.shape), fields[:2], fields[2:]


def solution(mesh):
    field = P("tiles", None)
    blocks = P(None, "tiles", "bins", None)
    whole = P("bins", "tiles", None)
    return jax.shard_map(
        shards,
        mesh=mesh,
        in_specs=(whole, field, field, field, field, field),
        out_specs=(whole, blocks, blocks),
        check_vma=False,
    )
```

```python
import math

import jax
import jax.numpy as jnp
import numpy as np
from jax import lax
from jax.experimental import pallas as pl
from jax.experimental.pallas import tpu as pltpu
from jax.sharding import PartitionSpec as P

NDIR = 36
NFREQ = 32
LON_BLOCKS = 16
STEPS = 4
COURANT_MAX = 0.6
GRID_STEP = 0.25 * math.pi / 180.0

ROWS = 8
NLON = 1440
BLK = 90
LANES = 128
TILES = 12
TAIL = NLON - (TILES - 1) * LANES
NF = 4
GROUPS = 9
G1 = 7
G2 = GROUPS - G1
TPG = NF * (TILES - 1) + 1

F32 = jnp.float32
PER_STEP = 2
LIMIT = 16 << 20
ANGLES = (np.arange(NDIR, dtype=np.float32) + 0.5) * np.float32(2.0 * math.pi / NDIR)
TRIG = np.concatenate([np.cos(ANGLES), np.sin(ANGLES)]).astype(np.float32)


def lane_iota():
    return lax.broadcasted_iota(jnp.int32, (ROWS, LANES), 1)


def sub_iota():
    return lax.broadcasted_iota(jnp.int32, (ROWS, LANES), 0)


def pack_group(src_ref, local, mask_ref, out_ref, group, upward, lane, low):
    def pair(j, i):
        cols = pl.ds(i * LANES, LANES)
        mask = mask_ref[:, cols].astype(F32)
        first = src_ref[j, 2 * local, :, cols] * mask
        second = src_ref[j, 2 * local + 1, :, cols] * mask
        if upward:
            return jnp.where(low, pltpu.roll(first, 4, 0), second)
        return jnp.where(low, first, pltpu.roll(second, 4, 0))

    for i in range(TILES - 1):
        for j in range(NF):
            out_ref[group, j * (TILES - 1) + i] = pair(j, i)
    tail = pair(0, TILES - 1)
    for j in range(1, NF):
        moved = pltpu.roll(pair(j, TILES - 1), TAIL * j, 1)
        tail = jnp.where(lane >= TAIL * j, moved, tail)
    out_ref[group, TPG - 1] = tail


def pack_kernel(base, width, with_mask, up_ref, src_ref, mask_ref, out_ref):
    lane = lane_iota()
    low = sub_iota() < 4
    upward = up_ref[0] == 1

    def fill(is_up):
        for u in range(width):
            g = pl.program_id(0) * width + u
            local = u if is_up else width - 1 - u
            pack_group(src_ref, local, mask_ref, out_ref, g, is_up, lane, low)
            if with_mask:
                start = jnp.minimum(g, TILES // 2 - 1) * (2 * LANES)
                start = pl.multiple_of(start, 2 * LANES)
                first = mask_ref[:, pl.ds(start, LANES)].astype(F32)
                second = mask_ref[:, pl.ds(start + LANES, LANES)].astype(F32)
                if is_up:
                    first = pltpu.roll(first, 4, 0)
                else:
                    second = pltpu.roll(second, 4, 0)
                out_ref[g, TPG] = jnp.where(low, first, second)

    pl.when(upward)(lambda: fill(True))
    pl.when(jnp.logical_not(upward))(lambda: fill(False))


def block_of(base, width, step, south):
    last = (2 * GROUPS - base) // width - 1
    return jnp.where(south == 1, base // width + step, last - step)


def pack(upward, spectral, sea_mask, base, groups, width, with_mask, name):
    tiles = TPG + 1 if with_mask else TPG
    block = (NF, 2 * width, ROWS, TILES * LANES)
    return pl.pallas_call(
        lambda *refs: pack_kernel(base, width, with_mask, *refs),
        grid_spec=pltpu.PrefetchScalarGridSpec(
            num_scalar_prefetch=1,
            grid=(groups // width,),
            in_specs=[
                pl.BlockSpec(
                    block, lambda g, up: (0, block_of(base, width, g, up[0]), 0, 0)
                ),
                pl.BlockSpec((ROWS, TILES * LANES), lambda g, up: (0, 0)),
            ],
            out_specs=pl.BlockSpec(memory_space=pltpu.VMEM),
        ),
        out_shape=pltpu.VMEM((groups, tiles, ROWS, LANES), F32),
        compiler_params=pltpu.CompilerParams(vmem_limit_bytes=LIMIT),
        name=name,
    )(upward, spectral, sea_mask)


WEST, EAST, BOTH = 0, 1, 2


def fill_wrap(tiles, lane):
    last = tiles[-1]
    after = pltpu.roll(tiles[0], TAIL, 1)
    before = pltpu.roll(last, LANES - TAIL, 1)
    filled = jnp.where(lane < LANES - TAIL, after, before)
    return tiles[:-1] + [jnp.where(lane < TAIL, last, filled)]


def shift_lanes(tiles, west, lane):
    if west:
        moved = [pltpu.roll(t, 1, 1) for t in tiles]
        return [jnp.where(lane == 0, moved[i - 1], moved[i]) for i in range(TILES)]
    moved = [pltpu.roll(t, LANES - 1, 1) for t in tiles]
    return [
        jnp.where(lane == LANES - 1, moved[(i + 1) % TILES], moved[i])
        for i in range(TILES)
    ]


def x_side(direction):
    west = direction < NDIR // 4 or direction >= NDIR - NDIR // 4
    return WEST if west else EAST


def pair_side(dp):
    first, second = x_side(2 * dp), x_side(2 * dp + 1)
    return first if first == second else BOTH


def run_cases(index, values, south_below, side_of, body):
    found = {}
    for v in values:
        found.setdefault((v < south_below, side_of(v)), []).append(v)
    for (south, side), members in sorted(found.items()):
        cond = index == members[0]
        for m in members[1:]:
            cond = jnp.logical_or(cond, index == m)
        pl.when(cond)(lambda south=south, side=side: body(south, side))


def load_tiles(ref):
    return [ref[:, pl.ds(i * LANES, LANES)].astype(F32) for i in range(TILES)]


def fill_metric(first_row, lat_total, out_ref):
    sub = sub_iota()
    part = sub % 4
    rows = [(sub, sub >= 0)]
    rows += [(part - 4 + k, part < 3) for k in range(1, STEPS + 1)]
    rows += [(part + ROWS - k, part > 0) for k in range(1, STEPS + 1)]
    edge = math.cos((lat_total / 2 - 0.5) * GRID_STEP)
    for n, (row, inside) in enumerate(rows):
        row = (first_row + row).astype(F32)
        latitude = (row - lat_total / 2 + 0.5) * GRID_STEP
        out_ref[n] = jnp.where(inside, edge / jnp.cos(latitude), 0.0)


def own_kernel(
    lat_total,
    tab_ref,
    trig_ref,
    row_ref,
    sea_ref,
    ice_ref,
    friction_ref,
    wind_ref,
    src_ref,
    out_ref,
    mask_ref,
    force_ref,
    met_ref,
):
    step = pl.program_id(0)
    lane = lane_iota()
    sub = sub_iota()

    @pl.when(step == 0)
    def _():
        sea = fill_wrap(load_tiles(sea_ref), lane)
        ice = load_tiles(ice_ref)
        friction = load_tiles(friction_ref)
        wind = load_tiles(wind_ref)
        for i in range(TILES):
            strength = 0.5 * friction[i] * friction[i]
            mask_ref[i] = sea[i]
            force_ref[0, i] = strength * jnp.cos(wind[i])
            force_ref[1, i] = strength * jnp.sin(wind[i])
            force_ref[2, i] = 1.0 - 0.5 * ice[i]
        fill_metric(row_ref[0], lat_total, met_ref)

    def one(local, carry):
        direction = 2 * PER_STEP * step + local

        def body(south, side):
            west = side == WEST
            inflow = sub > 0 if south else sub < ROWS - 1
            fields = []
            coefs = []
            for j in range(NF):
                cy = tab_ref[j] * jnp.abs(trig_ref[NDIR + direction])
                cx = tab_ref[j] * jnp.abs(trig_ref[direction]) * met_ref[0]
                alpha = 1.0 - cx - cy
                coefs.append((alpha, cx, jnp.where(inflow, cy, 0.0)))
                tiles = [
                    src_ref[j, local, :, pl.ds(i * LANES, LANES)] for i in range(TILES)
                ]
                tiles = fill_wrap(tiles, lane)
                fields.append([t * mask_ref[i] for i, t in enumerate(tiles)])
            for sub_step in range(STEPS):
                new = []
                for tiles, (alpha, cx, cy) in zip(fields, coefs):
                    xs = shift_lanes(tiles, west, lane)
                    done = []
                    for i in range(TILES):
                        y = pltpu.roll(tiles[i], 1 if south else ROWS - 1, 0)
                        total = alpha * tiles[i] + cx * xs[i] + cy * y
                        done.append(total * mask_ref[i])
                    new.append(done)
                fields = new
            for j in range(NF):
                for i in range(TILES):
                    out_ref[local // 2, local % 2, j, i] = fields[j][i]

        run_cases(direction, range(NDIR), NDIR // 2, x_side, body)
        return carry

    lax.fori_loop(0, 2 * PER_STEP, one, 0)


def own_rows(
    spectral, table, trig, first_row, lat_total, sea_mask, ice_mask, friction, wind_dir
):
    whole = pl.BlockSpec(memory_space=pltpu.VMEM)
    field = pl.BlockSpec((ROWS, TILES * LANES), lambda i: (0, 0))
    return pl.pallas_call(
        lambda *refs: own_kernel(lat_total, *refs),
        grid=(2 * GROUPS // PER_STEP,),
        in_specs=[
            pl.BlockSpec(memory_space=pltpu.SMEM),
            pl.BlockSpec(memory_space=pltpu.SMEM),
            pl.BlockSpec(memory_space=pltpu.SMEM),
            field,
            field,
            field,
            field,
            pl.BlockSpec(
                (NF, 2 * PER_STEP, ROWS, TILES * LANES), lambda i: (0, i, 0, 0)
            ),
        ],
        out_specs=[
            pl.BlockSpec(
                (PER_STEP, 2, NF, TILES, ROWS, LANES), lambda i: (i, 0, 0, 0, 0, 0)
            ),
            whole,
            whole,
            whole,
        ],
        out_shape=[
            jax.ShapeDtypeStruct((2 * GROUPS, 2, NF, TILES, ROWS, LANES), F32),
            pltpu.VMEM((TILES, ROWS, LANES), F32),
            pltpu.VMEM((3, TILES, ROWS, LANES), F32),
            pltpu.VMEM((1 + 2 * STEPS, ROWS, LANES), F32),
        ],
        compiler_params=pltpu.CompilerParams(vmem_limit_bytes=LIMIT),
        name="own",
    )(table, trig, first_row, sea_mask, ice_mask, friction, wind_dir, spectral)


def window_masks(south, mask_ref, halo_ref, out_ref, lane, low):
    rows = []
    for i in range(TILES):
        edge = halo_ref[i // 2, 0]
        if (i % 2 == 0) != south:
            edge = pltpu.roll(edge, 4, 0)
        mine = pltpu.roll(mask_ref[i], 4, 0)
        if south:
            rows.append(jnp.where(low, edge, mine))
        else:
            rows.append(jnp.where(low, mine, edge))
    rows = fill_wrap(rows, lane)
    for k in range(1, STEPS + 1):
        first = k if south else 4 - k
        for i in range(TILES):
            window = rows[i]
            if first > 0:
                window = pltpu.roll(window, ROWS - first, 0)
            out_ref[k - 1, i] = jnp.where(low, window, pltpu.roll(window, 4, 0))


def finish_kernel(
    base,
    groups,
    width,
    south_ref,
    tab_ref,
    trig_ref,
    met_ref,
    mask_ref,
    wind_ref,
    own_ref,
    halo_ref,
    edge_ref,
    prev_ref,
    old_ref,
    out_ref,
    acc_ref,
    win_ref,
    c_ref,
):
    step = pl.program_id(0)
    is_south = south_ref[0] == 1
    dps = [base + g for g in range(groups)]
    dps = dps + [2 * GROUPS - 1 - d for d in dps]
    lane = lane_iota()
    sub = sub_iota()
    low = sub < 4

    @pl.when(step == 0)
    def _():
        if prev_ref is None:
            acc_ref[...] = jnp.zeros_like(acc_ref)
        else:
            acc_ref[...] = prev_ref[...]

    if edge_ref is not None:
        for south in (True, False):
            mine = jnp.logical_and(step == 0, is_south == south)
            pl.when(mine)(
                lambda south=south: window_masks(
                    south, mask_ref, edge_ref, win_ref, lane, low
                )
            )

    windows = mask_ref if edge_ref is None else win_ref

    def one(u, carry):
        local = jnp.where(is_south, u, width - 1 - u)
        group = base + step * width + u
        dp = jnp.where(is_south, group, 2 * GROUPS - 1 - group)

        def contribution(south, side):
            row = 0 if south else 1
            fields = []
            scalars = []
            for j in range(NF):
                courant = tab_ref[j]
                bx = courant * jnp.abs(
                    jnp.where(low, trig_ref[2 * dp], trig_ref[2 * dp + 1])
                )
                cy = courant * jnp.abs(
                    jnp.where(low, trig_ref[NDIR + 2 * dp], trig_ref[NDIR + 2 * dp + 1])
                )
                inside = sub % 4 < 3 if south else sub % 4 > 0
                scalars.append((bx, cy, jnp.where(inside, 1.0 - cy, 0.0)))
                tiles = [halo_ref[u, j * (TILES - 1) + i] for i in range(TILES - 1)]
                last = halo_ref[u, TPG - 1]
                if j > 0:
                    last = pltpu.roll(last, LANES - TAIL * j, 1)
                fields.append(fill_wrap(tiles + [last], lane))
            for k in range(STEPS):
                new = []
                for tiles, (bx, cy, rest) in zip(fields, scalars):
                    cx = bx * met_ref[1 + row * STEPS + k]
                    alpha = rest - cx
                    ahead = [pltpu.roll(t, ROWS - 1 if south else 1, 0) for t in tiles]
                    if side == BOTH:
                        west = shift_lanes(ahead, True, lane)
                        east = shift_lanes(ahead, False, lane)
                        here = low if south else jnp.logical_not(low)
                        xs = [jnp.where(here, w, e) for w, e in zip(west, east)]
                    else:
                        xs = shift_lanes(ahead, side == WEST, lane)
                    new.append(
                        [
                            (alpha * ahead[i] + cx * xs[i] + cy * tiles[i])
                            * windows[k, i]
                            for i in range(TILES)
                        ]
                    )
                fields = new
            for j in range(NF):
                for i in range(TILES):
                    c_ref[j, i] = fields[j][i]

        run_cases(dp, dps, GROUPS, pair_side, contribution)

        def combine(south, side):
            weight = [tab_ref[NF + j] for j in range(NF)]
            angle = [
                (trig_ref[2 * dp + dd], trig_ref[NDIR + 2 * dp + dd]) for dd in range(2)
            ]
            target = low if south else jnp.logical_not(low)
            for first in range(0, TILES, 2):
                held = []
                for i in (first, first + 1):
                    held.append(
                        (
                            [wind_ref[n, i] for n in range(3)],
                            [c_ref[j, i] for j in range(NF)],
                            [acc_ref[n, i] for n in range(4)],
                            [
                                [own_ref[local, dd, j, i] for j in range(NF)]
                                for dd in range(2)
                            ],
                        )
                    )
                results = []
                for (east, north, ice), parts, total, own in held:
                    made = []
                    for dd in range(2):
                        cos_d, sin_d = angle[dd]
                        h = jnp.maximum(cos_d * east + sin_d * north, 0.0)
                        for j in range(NF):
                            c = parts[j]
                            if (dd == 0) != south:
                                c = pltpu.roll(c, 4, 0)
                            e = own[dd][j] + jnp.where(target, c, 0.0)
                            x = weight[j] * e
                            made.append((e + h * x) * ice)
                            y = weight[j] * x
                            sum_x = x if j == 0 else sum_x + x
                            sum_y = y if j == 0 else sum_y + y
                        source = h * sum_x
                        drift = ice * (sum_x + h * sum_y)
                        total = [
                            total[0] + cos_d * drift,
                            total[1] + sin_d * drift,
                            total[2] + cos_d * source,
                            total[3] + sin_d * source,
                        ]
                    results.append((made, total))
                for i, (made, total) in zip((first, first + 1), results):
                    cols = pl.ds(i * LANES, LANES)
                    for dd in range(2):
                        for j in range(NF):
                            out_ref[j, 2 * local + dd, :, cols] = made[dd * NF + j]
                    for n in range(4):
                        acc_ref[n, i] = total[n]

        run_cases(dp, dps, GROUPS, lambda d: WEST, combine)
        return carry

    lax.fori_loop(0, width, one, 0)


def in_vmem(x):
    return pltpu.with_memory_space_constraint(x, pltpu.VMEM)


def in_hbm(x):
    return pltpu.with_memory_space_constraint(x, pltpu.HBM)


def finish(south, table, trig, metric, mask, wind, own, halo, prev, old, base, width, name):
    groups, tiles = halo.shape[:2]
    whole = pl.BlockSpec(memory_space=pltpu.VMEM)
    block = lambda i, s: block_of(base, width, i, s[0])
    in_specs = [
        pl.BlockSpec(memory_space=pltpu.SMEM),
        pl.BlockSpec(memory_space=pltpu.SMEM),
        whole,
        whole,
        whole,
        pl.BlockSpec(
            (width, 2, NF, TILES, ROWS, LANES),
            lambda i, s: (block(i, s), 0, 0, 0, 0, 0),
        ),
        pl.BlockSpec((width, tiles, ROWS, LANES), lambda i, s: (i, 0, 0, 0)),
    ]
    halo = in_hbm(halo)
    args = [south, table, trig, in_vmem(metric), in_vmem(mask), in_vmem(wind)]
    args += [own, halo]
    out_specs = [
        pl.BlockSpec(
            (NF, 2 * width, ROWS, TILES * LANES), lambda i, s: (0, block(i, s), 0, 0)
        ),
        whole,
    ]
    out_shape = [
        jax.ShapeDtypeStruct((NF, NDIR, ROWS, NLON), F32),
        pltpu.VMEM((4, TILES, ROWS, LANES), F32),
    ]
    with_edge = tiles > TPG
    with_prev = prev is not None
    aliases = {}
    if with_edge:
        in_specs.append(
            pl.BlockSpec((TILES // 2, 1, ROWS, LANES), lambda i, s: (0, TPG, 0, 0))
        )
        args.append(halo)
        out_specs.append(whole)
        out_shape.append(pltpu.VMEM((STEPS, TILES, ROWS, LANES), F32))
    if with_prev:
        in_specs += [whole, pl.BlockSpec(memory_space=pl.ANY)]
        args += [in_vmem(prev), old]
        aliases = {len(args) - 1: 0}

    def kernel(*refs):
        refs = list(refs)
        fixed, refs = refs[:8], refs[8:]
        edge = refs.pop(0) if with_edge else None
        before = refs.pop(0) if with_prev else None
        former = refs.pop(0) if with_prev else None
        result, acc = refs.pop(0), refs.pop(0)
        windows = refs.pop(0) if with_edge else None
        finish_kernel(
            base,
            groups,
            width,
            *fixed,
            edge,
            before,
            former,
            result,
            acc,
            windows,
            *refs,
        )

    return pl.pallas_call(
        kernel,
        grid_spec=pltpu.PrefetchScalarGridSpec(
            num_scalar_prefetch=1,
            grid=(groups // width,),
            in_specs=in_specs,
            out_specs=out_specs,
            scratch_shapes=[pltpu.VMEM((NF, TILES, ROWS, LANES), F32)],
        ),
        out_shape=out_shape,
        input_output_aliases=aliases,
        compiler_params=pltpu.CompilerParams(vmem_limit_bytes=LIMIT),
        name=name,
    )(*args)


def slots_kernel(owner_ref, acc_ref, out_ref, order_ref, count_ref):
    lane = lane_iota()
    for k in range(LON_BLOCKS // 2):
        count_ref[k] = 0
    for block in range(LON_BLOCKS):
        owner = owner_ref[0, block]
        seen = count_ref[owner]
        order_ref[2 * owner + seen] = block
        count_ref[owner] = seen + 1

    for k in range(LON_BLOCKS // 2):
        rests = []
        for c in range(4):
            parts = []
            for s in range(2):
                column = order_ref[2 * k + s] * BLK
                tile = column // LANES
                shift = column % LANES
                back = (LANES - shift) % LANES
                here = pltpu.roll(acc_ref[c, tile], back, 1)
                after = pltpu.roll(acc_ref[c, jnp.minimum(tile + 1, TILES - 1)], back, 1)
                parts.append(jnp.where(lane < LANES - shift, here, after))
            moved = pltpu.roll(parts[1], BLK, 1)
            out_ref[k, c] = jnp.where(lane < BLK, parts[0], moved)
            rests.append(moved)
        for c in range(2):
            other = pltpu.roll(rests[2 * c + 1], LANES // 2, 1)
            both = jnp.where(lane < LANES // 2, rests[2 * c], other)
            used = lane % (LANES // 2) < 2 * BLK - LANES
            out_ref[k, 4 + c] = jnp.where(used, both, 0.0)


def pick_slots(owner, acc):
    return pl.pallas_call(
        slots_kernel,
        in_specs=[
            pl.BlockSpec(memory_space=pltpu.SMEM),
            pl.BlockSpec(memory_space=pltpu.VMEM),
        ],
        out_specs=pl.BlockSpec(memory_space=pltpu.VMEM),
        out_shape=pltpu.VMEM((LON_BLOCKS // 2, 6, ROWS, LANES), F32),
        scratch_shapes=[
            pltpu.SMEM((LON_BLOCKS,), jnp.int32),
            pltpu.SMEM((LON_BLOCKS // 2,), jnp.int32),
        ],
        compiler_params=pltpu.CompilerParams(vmem_limit_bytes=LIMIT),
        name="slots",
    )(owner, acc)


def shards(spectrum, sea_mask, ice_mask, friction, wind_dir, ocean_owner):
    count = lax.axis_size("tiles")
    first_row = (lax.axis_index("tiles") * ROWS).astype(jnp.int32).reshape(1)
    spectral = in_hbm(spectrum.reshape(NF, NDIR, ROWS, NLON))
    sea = in_hbm(sea_mask)
    odd = lax.axis_index("tiles") % 2
    odd = odd.astype(jnp.int32).reshape(1)
    even = 1 - odd

    def swap(x, start):
        pairs = [(i, i + 1) for i in range(start, count - 1, 2)]
        return lax.ppermute(x, "tiles", pairs + [(j, i) for i, j in pairs])

    near = pack(even, spectral, sea, 0, GROUPS, 3, True, "near")
    sea, _ = lax.optimization_barrier((sea, near))
    near = swap(near, 0)
    far1 = pack(odd, spectral, sea, 0, G1, 1, True, "far1")
    sea, _ = lax.optimization_barrier((sea, far1))
    far1 = swap(far1, 1)
    far2 = pack(odd, spectral, sea, G1, G2, 1, False, "far2")
    far2 = swap(far2, 1)

    place = np.tile(np.arange(NF), 2)
    speeds = np.arange(2 * NF) < NF
    freq_pos = (lax.axis_index("bins") * NF + place).astype(F32)
    power = jnp.where(speeds, -freq_pos, freq_pos - (NFREQ - 1))
    table = jnp.power(jnp.where(speeds, 1.1, 1.03).astype(F32), power)
    table = table * jnp.where(speeds, COURANT_MAX, 1.0).astype(F32)
    trig = jnp.asarray(TRIG)

    own, mask, wind, metric = own_rows(
        spectral,
        table,
        trig,
        first_row,
        count * ROWS,
        sea,
        ice_mask,
        friction,
        wind_dir,
    )
    common = (table, trig, metric)
    out, acc, _ = finish(
        odd, *common, mask, wind, own, near, None, None, 0, 3, "finish_near"
    )
    out, acc, windows = finish(
        even, *common, mask, wind, own, far1, acc, out, 0, 1, "finish_far1"
    )
    out, acc = finish(
        even, *common, windows, wind, own, far2, acc, out, G1, 1, "finish_far2"
    )

    sent = pick_slots(ocean_owner, acc)
    got = lax.all_to_all(sent, "bins", 0, 0, tiled=True)
    total = got.sum(0)
    rest = total[4:].reshape(2, ROWS, 2, LANES // 2).transpose(0, 2, 1, 3)
    rest = rest.reshape(4, ROWS, LANES // 2)[:, :, : 2 * BLK - LANES]
    fields = jnp.concatenate([total[:4], rest], axis=2).reshape(4, ROWS, 2, BLK)
    return out.reshape(spectrum.shape), fields[:2], fields[2:]


def solution(mesh):
    field = P("tiles", None)
    blocks = P(None, "tiles", "bins", None)
    whole = P("bins", "tiles", None)
    return jax.shard_map(
        shards,
        mesh=mesh,
        in_specs=(whole, field, field, field, field, field),
        out_specs=(whole, blocks, blocks),
        check_vma=False,
    )
```

```python
import math

import jax
import jax.numpy as jnp
import numpy as np
from jax import lax
from jax.experimental import pallas as pl
from jax.experimental.pallas import tpu as pltpu
from jax.sharding import PartitionSpec as P

NDIR = 36
NFREQ = 32
LON_BLOCKS = 16
STEPS = 4
COURANT_MAX = 0.6
GRID_STEP = 0.25 * math.pi / 180.0

ROWS = 8
NLON = 1440
BLK = 90
LANES = 128
TILES = 12
TAIL = NLON - (TILES - 1) * LANES
NF = 4
GROUPS = 9
G1 = 7
G2 = GROUPS - G1
TPG = NF * (TILES - 1) + 1

F32 = jnp.float32
PER_STEP = 3
LIMIT = 16 << 20
ANGLES = (np.arange(NDIR, dtype=np.float32) + 0.5) * np.float32(2.0 * math.pi / NDIR)
TRIG = np.concatenate([np.cos(ANGLES), np.sin(ANGLES)]).astype(np.float32)


def lane_iota():
    return lax.broadcasted_iota(jnp.int32, (ROWS, LANES), 1)


def sub_iota():
    return lax.broadcasted_iota(jnp.int32, (ROWS, LANES), 0)


def pack_group(src_ref, local, mask_ref, out_ref, group, upward, lane, low):
    def pair(j, i):
        cols = pl.ds(i * LANES, LANES)
        mask = mask_ref[:, cols].astype(F32)
        first = src_ref[j, 2 * local, :, cols] * mask
        second = src_ref[j, 2 * local + 1, :, cols] * mask
        if upward:
            return jnp.where(low, pltpu.roll(first, 4, 0), second)
        return jnp.where(low, first, pltpu.roll(second, 4, 0))

    for i in range(TILES - 1):
        for j in range(NF):
            out_ref[group, j * (TILES - 1) + i] = pair(j, i)
    tail = pair(0, TILES - 1)
    for j in range(1, NF):
        moved = pltpu.roll(pair(j, TILES - 1), TAIL * j, 1)
        tail = jnp.where(lane >= TAIL * j, moved, tail)
    out_ref[group, TPG - 1] = tail


def pack_kernel(base, width, with_mask, up_ref, src_ref, mask_ref, out_ref):
    lane = lane_iota()
    low = sub_iota() < 4
    upward = up_ref[0] == 1

    def fill(is_up):
        for u in range(width):
            g = pl.program_id(0) * width + u
            local = u if is_up else width - 1 - u
            pack_group(src_ref, local, mask_ref, out_ref, g, is_up, lane, low)
            if with_mask:
                start = jnp.minimum(g, TILES // 2 - 1) * (2 * LANES)
                start = pl.multiple_of(start, 2 * LANES)
                first = mask_ref[:, pl.ds(start, LANES)].astype(F32)
                second = mask_ref[:, pl.ds(start + LANES, LANES)].astype(F32)
                if is_up:
                    first = pltpu.roll(first, 4, 0)
                else:
                    second = pltpu.roll(second, 4, 0)
                out_ref[g, TPG] = jnp.where(low, first, second)

    pl.when(upward)(lambda: fill(True))
    pl.when(jnp.logical_not(upward))(lambda: fill(False))


def block_of(base, width, step, south):
    last = (2 * GROUPS - base) // width - 1
    return jnp.where(south == 1, base // width + step, last - step)


def pack(upward, spectral, sea_mask, base, groups, width, with_mask, name):
    tiles = TPG + 1 if with_mask else TPG
    block = (NF, 2 * width, ROWS, TILES * LANES)
    return pl.pallas_call(
        lambda *refs: pack_kernel(base, width, with_mask, *refs),
        grid_spec=pltpu.PrefetchScalarGridSpec(
            num_scalar_prefetch=1,
            grid=(groups // width,),
            in_specs=[
                pl.BlockSpec(
                    block, lambda g, up: (0, block_of(base, width, g, up[0]), 0, 0)
                ),
                pl.BlockSpec((ROWS, TILES * LANES), lambda g, up: (0, 0)),
            ],
            out_specs=pl.BlockSpec(memory_space=pltpu.VMEM),
        ),
        out_shape=pltpu.VMEM((groups, tiles, ROWS, LANES), F32),
        compiler_params=pltpu.CompilerParams(vmem_limit_bytes=LIMIT),
        name=name,
    )(upward, spectral, sea_mask)


WEST, EAST, BOTH = 0, 1, 2


def fill_wrap(tiles, lane):
    last = tiles[-1]
    after = pltpu.roll(tiles[0], TAIL, 1)
    before = pltpu.roll(last, LANES - TAIL, 1)
    filled = jnp.where(lane < LANES - TAIL, after, before)
    return tiles[:-1] + [jnp.where(lane < TAIL, last, filled)]


def shift_lanes(tiles, west, lane):
    if west:
        moved = [pltpu.roll(t, 1, 1) for t in tiles]
        return [jnp.where(lane == 0, moved[i - 1], moved[i]) for i in range(TILES)]
    moved = [pltpu.roll(t, LANES - 1, 1) for t in tiles]
    return [
        jnp.where(lane == LANES - 1, moved[(i + 1) % TILES], moved[i])
        for i in range(TILES)
    ]


def x_side(direction):
    west = direction < NDIR // 4 or direction >= NDIR - NDIR // 4
    return WEST if west else EAST


def pair_side(dp):
    first, second = x_side(2 * dp), x_side(2 * dp + 1)
    return first if first == second else BOTH


def run_cases(index, values, south_below, side_of, body):
    found = {}
    for v in values:
        found.setdefault((v < south_below, side_of(v)), []).append(v)
    for (south, side), members in sorted(found.items()):
        cond = index == members[0]
        for m in members[1:]:
            cond = jnp.logical_or(cond, index == m)
        pl.when(cond)(lambda south=south, side=side: body(south, side))


def load_tiles(ref):
    return [ref[:, pl.ds(i * LANES, LANES)].astype(F32) for i in range(TILES)]


def fill_metric(first_row, lat_total, out_ref):
    sub = sub_iota()
    part = sub % 4
    rows = [(sub, sub >= 0)]
    rows += [(part - 4 + k, part < 3) for k in range(1, STEPS + 1)]
    rows += [(part + ROWS - k, part > 0) for k in range(1, STEPS + 1)]
    edge = math.cos((lat_total / 2 - 0.5) * GRID_STEP)
    for n, (row, inside) in enumerate(rows):
        row = (first_row + row).astype(F32)
        latitude = (row - lat_total / 2 + 0.5) * GRID_STEP
        out_ref[n] = jnp.where(inside, edge / jnp.cos(latitude), 0.0)


def own_kernel(
    lat_total,
    tab_ref,
    trig_ref,
    row_ref,
    sea_ref,
    ice_ref,
    friction_ref,
    wind_ref,
    src_ref,
    out_ref,
    mask_ref,
    force_ref,
    met_ref,
):
    step = pl.program_id(0)
    lane = lane_iota()
    sub = sub_iota()

    @pl.when(step == 0)
    def _():
        sea = fill_wrap(load_tiles(sea_ref), lane)
        ice = load_tiles(ice_ref)
        friction = load_tiles(friction_ref)
        wind = load_tiles(wind_ref)
        for i in range(TILES):
            strength = 0.5 * friction[i] * friction[i]
            mask_ref[i] = sea[i]
            force_ref[0, i] = strength * jnp.cos(wind[i])
            force_ref[1, i] = strength * jnp.sin(wind[i])
            force_ref[2, i] = 1.0 - 0.5 * ice[i]
        fill_metric(row_ref[0], lat_total, met_ref)

    def one(local, carry):
        direction = 2 * PER_STEP * step + local

        def body(south, side):
            west = side == WEST
            inflow = sub > 0 if south else sub < ROWS - 1
            fields = []
            coefs = []
            for j in range(NF):
                cy = tab_ref[j] * jnp.abs(trig_ref[NDIR + direction])
                cx = tab_ref[j] * jnp.abs(trig_ref[direction]) * met_ref[0]
                alpha = 1.0 - cx - cy
                coefs.append((alpha, cx, jnp.where(inflow, cy, 0.0)))
                tiles = [
                    src_ref[j, local, :, pl.ds(i * LANES, LANES)] for i in range(TILES)
                ]
                tiles = fill_wrap(tiles, lane)
                fields.append([t * mask_ref[i] for i, t in enumerate(tiles)])
            for sub_step in range(STEPS):
                new = []
                for tiles, (alpha, cx, cy) in zip(fields, coefs):
                    xs = shift_lanes(tiles, west, lane)
                    done = []
                    for i in range(TILES):
                        y = pltpu.roll(tiles[i], 1 if south else ROWS - 1, 0)
                        total = alpha * tiles[i] + cx * xs[i] + cy * y
                        done.append(total * mask_ref[i])
                    new.append(done)
                fields = new
            for j in range(NF):
                for i in range(TILES):
                    out_ref[local // 2, local % 2, j, i] = fields[j][i]

        run_cases(direction, range(NDIR), NDIR // 2, x_side, body)
        return carry

    lax.fori_loop(0, 2 * PER_STEP, one, 0)


def own_rows(
    spectral, table, trig, first_row, lat_total, sea_mask, ice_mask, friction, wind_dir
):
    whole = pl.BlockSpec(memory_space=pltpu.VMEM)
    field = pl.BlockSpec((ROWS, TILES * LANES), lambda i: (0, 0))
    return pl.pallas_call(
        lambda *refs: own_kernel(lat_total, *refs),
        grid=(2 * GROUPS // PER_STEP,),
        in_specs=[
            pl.BlockSpec(memory_space=pltpu.SMEM),
            pl.BlockSpec(memory_space=pltpu.SMEM),
            pl.BlockSpec(memory_space=pltpu.SMEM),
            field,
            field,
            field,
            field,
            pl.BlockSpec(
                (NF, 2 * PER_STEP, ROWS, TILES * LANES), lambda i: (0, i, 0, 0)
            ),
        ],
        out_specs=[
            pl.BlockSpec(
                (PER_STEP, 2, NF, TILES, ROWS, LANES), lambda i: (i, 0, 0, 0, 0, 0)
            ),
            whole,
            whole,
            whole,
        ],
        out_shape=[
            jax.ShapeDtypeStruct((2 * GROUPS, 2, NF, TILES, ROWS, LANES), F32),
            pltpu.VMEM((TILES, ROWS, LANES), F32),
            pltpu.VMEM((3, TILES, ROWS, LANES), F32),
            pltpu.VMEM((1 + 2 * STEPS, ROWS, LANES), F32),
        ],
        compiler_params=pltpu.CompilerParams(vmem_limit_bytes=LIMIT),
        name="own",
    )(table, trig, first_row, sea_mask, ice_mask, friction, wind_dir, spectral)


def window_masks(south, mask_ref, halo_ref, out_ref, lane, low):
    rows = []
    for i in range(TILES):
        edge = halo_ref[i // 2, 0]
        if (i % 2 == 0) != south:
            edge = pltpu.roll(edge, 4, 0)
        mine = pltpu.roll(mask_ref[i], 4, 0)
        if south:
            rows.append(jnp.where(low, edge, mine))
        else:
            rows.append(jnp.where(low, mine, edge))
    rows = fill_wrap(rows, lane)
    for k in range(1, STEPS + 1):
        first = k if south else 4 - k
        for i in range(TILES):
            window = rows[i]
            if first > 0:
                window = pltpu.roll(window, ROWS - first, 0)
            out_ref[k - 1, i] = jnp.where(low, window, pltpu.roll(window, 4, 0))


def finish_kernel(
    base,
    groups,
    width,
    south_ref,
    tab_ref,
    trig_ref,
    met_ref,
    mask_ref,
    wind_ref,
    own_ref,
    halo_ref,
    edge_ref,
    prev_ref,
    old_ref,
    out_ref,
    acc_ref,
    win_ref,
    c_ref,
):
    step = pl.program_id(0)
    is_south = south_ref[0] == 1
    dps = [base + g for g in range(groups)]
    dps = dps + [2 * GROUPS - 1 - d for d in dps]
    lane = lane_iota()
    sub = sub_iota()
    low = sub < 4

    @pl.when(step == 0)
    def _():
        if prev_ref is None:
            acc_ref[...] = jnp.zeros_like(acc_ref)
        else:
            acc_ref[...] = prev_ref[...]

    if edge_ref is not None:
        for south in (True, False):
            mine = jnp.logical_and(step == 0, is_south == south)
            pl.when(mine)(
                lambda south=south: window_masks(
                    south, mask_ref, edge_ref, win_ref, lane, low
                )
            )

    windows = mask_ref if edge_ref is None else win_ref

    def one(u, carry):
        local = jnp.where(is_south, u, width - 1 - u)
        group = base + step * width + u
        dp = jnp.where(is_south, group, 2 * GROUPS - 1 - group)

        def contribution(south, side):
            row = 0 if south else 1
            fields = []
            scalars = []
            for j in range(NF):
                courant = tab_ref[j]
                bx = courant * jnp.abs(
                    jnp.where(low, trig_ref[2 * dp], trig_ref[2 * dp + 1])
                )
                cy = courant * jnp.abs(
                    jnp.where(low, trig_ref[NDIR + 2 * dp], trig_ref[NDIR + 2 * dp + 1])
                )
                inside = sub % 4 < 3 if south else sub % 4 > 0
                scalars.append((bx, cy, jnp.where(inside, 1.0 - cy, 0.0)))
                tiles = [halo_ref[u, j * (TILES - 1) + i] for i in range(TILES - 1)]
                last = halo_ref[u, TPG - 1]
                if j > 0:
                    last = pltpu.roll(last, LANES - TAIL * j, 1)
                fields.append(fill_wrap(tiles + [last], lane))
            for k in range(STEPS):
                new = []
                for tiles, (bx, cy, rest) in zip(fields, scalars):
                    cx = bx * met_ref[1 + row * STEPS + k]
                    alpha = rest - cx
                    ahead = [pltpu.roll(t, ROWS - 1 if south else 1, 0) for t in tiles]
                    if side == BOTH:
                        west = shift_lanes(ahead, True, lane)
                        east = shift_lanes(ahead, False, lane)
                        here = low if south else jnp.logical_not(low)
                        xs = [jnp.where(here, w, e) for w, e in zip(west, east)]
                    else:
                        xs = shift_lanes(ahead, side == WEST, lane)
                    new.append(
                        [
                            (alpha * ahead[i] + cx * xs[i] + cy * tiles[i])
                            * windows[k, i]
                            for i in range(TILES)
                        ]
                    )
                fields = new
            for j in range(NF):
                for i in range(TILES):
                    c_ref[j, i] = fields[j][i]

        run_cases(dp, dps, GROUPS, pair_side, contribution)

        def combine(south, side):
            weight = [tab_ref[NF + j] for j in range(NF)]
            angle = [
                (trig_ref[2 * dp + dd], trig_ref[NDIR + 2 * dp + dd]) for dd in range(2)
            ]
            target = low if south else jnp.logical_not(low)
            for first in range(0, TILES, 2):
                held = []
                for i in (first, first + 1):
                    held.append(
                        (
                            [wind_ref[n, i] for n in range(3)],
                            [c_ref[j, i] for j in range(NF)],
                            [acc_ref[n, i] for n in range(4)],
                            [
                                [own_ref[local, dd, j, i] for j in range(NF)]
                                for dd in range(2)
                            ],
                        )
                    )
                results = []
                for (east, north, ice), parts, total, own in held:
                    made = []
                    for dd in range(2):
                        cos_d, sin_d = angle[dd]
                        h = jnp.maximum(cos_d * east + sin_d * north, 0.0)
                        for j in range(NF):
                            c = parts[j]
                            if (dd == 0) != south:
                                c = pltpu.roll(c, 4, 0)
                            e = own[dd][j] + jnp.where(target, c, 0.0)
                            x = weight[j] * e
                            made.append((e + h * x) * ice)
                            y = weight[j] * x
                            sum_x = x if j == 0 else sum_x + x
                            sum_y = y if j == 0 else sum_y + y
                        source = h * sum_x
                        drift = ice * (sum_x + h * sum_y)
                        total = [
                            total[0] + cos_d * drift,
                            total[1] + sin_d * drift,
                            total[2] + cos_d * source,
                            total[3] + sin_d * source,
                        ]
                    results.append((made, total))
                for i, (made, total) in zip((first, first + 1), results):
                    cols = pl.ds(i * LANES, LANES)
                    for dd in range(2):
                        for j in range(NF):
                            out_ref[j, 2 * local + dd, :, cols] = made[dd * NF + j]
                    for n in range(4):
                        acc_ref[n, i] = total[n]

        run_cases(dp, dps, GROUPS, lambda d: WEST, combine)
        return carry

    lax.fori_loop(0, width, one, 0)


def slots_kernel(owner_ref, acc_ref, out_ref, order_ref, count_ref):
    lane = lane_iota()
    for k in range(LON_BLOCKS // 2):
        count_ref[k] = 0
    for block in range(LON_BLOCKS):
        owner = owner_ref[0, block]
        seen = count_ref[owner]
        order_ref[2 * owner + seen] = block
        count_ref[owner] = seen + 1

    for k in range(LON_BLOCKS // 2):
        rests = []
        for c in range(4):
            parts = []
            for s in range(2):
                column = order_ref[2 * k + s] * BLK
                tile = column // LANES
                shift = column % LANES
                back = (LANES - shift) % LANES
                here = pltpu.roll(acc_ref[c, tile], back, 1)
                after = pltpu.roll(acc_ref[c, jnp.minimum(tile + 1, TILES - 1)], back, 1)
                parts.append(jnp.where(lane < LANES - shift, here, after))
            moved = pltpu.roll(parts[1], BLK, 1)
            out_ref[k, c] = jnp.where(lane < BLK, parts[0], moved)
            rests.append(moved)
        for c in range(2):
            other = pltpu.roll(rests[2 * c + 1], LANES // 2, 1)
            both = jnp.where(lane < LANES // 2, rests[2 * c], other)
            used = lane % (LANES // 2) < 2 * BLK - LANES
            out_ref[k, 4 + c] = jnp.where(used, both, 0.0)


def in_vmem(x):
    return pltpu.with_memory_space_constraint(x, pltpu.VMEM)


def in_hbm(x):
    return pltpu.with_memory_space_constraint(x, pltpu.HBM)


def finish(
    south,
    table,
    trig,
    metric,
    mask,
    wind,
    own,
    halo,
    prev,
    old,
    owner,
    base,
    width,
    name,
):
    groups, tiles = halo.shape[:2]
    whole = pl.BlockSpec(memory_space=pltpu.VMEM)
    block = lambda i, s: block_of(base, width, i, s[0])
    in_specs = [
        pl.BlockSpec(memory_space=pltpu.SMEM),
        pl.BlockSpec(memory_space=pltpu.SMEM),
        whole,
        whole,
        whole,
        pl.BlockSpec(
            (width, 2, NF, TILES, ROWS, LANES),
            lambda i, s: (block(i, s), 0, 0, 0, 0, 0),
        ),
        pl.BlockSpec((width, tiles, ROWS, LANES), lambda i, s: (i, 0, 0, 0)),
    ]
    halo = in_hbm(halo)
    args = [south, table, trig, in_vmem(metric), in_vmem(mask), in_vmem(wind)]
    args += [own, halo]
    out_specs = [
        pl.BlockSpec(
            (NF, 2 * width, ROWS, TILES * LANES), lambda i, s: (0, block(i, s), 0, 0)
        )
    ]
    out_shape = [jax.ShapeDtypeStruct((NF, NDIR, ROWS, NLON), F32)]
    acc_type = pltpu.VMEM((4, TILES, ROWS, LANES), F32)
    window_type = pltpu.VMEM((STEPS, TILES, ROWS, LANES), F32)
    scratch = [pltpu.VMEM((NF, TILES, ROWS, LANES), F32)]
    with_slots = owner is not None
    if with_slots:
        scratch.append(acc_type)
    else:
        out_specs.append(whole)
        out_shape.append(acc_type)
    with_edge = tiles > TPG
    with_prev = prev is not None
    aliases = {}
    if with_edge:
        in_specs.append(
            pl.BlockSpec((TILES // 2, 1, ROWS, LANES), lambda i, s: (0, TPG, 0, 0))
        )
        args.append(halo)
        if with_prev:
            out_specs.append(whole)
            out_shape.append(window_type)
        else:
            scratch.append(window_type)
    if with_prev:
        in_specs += [whole, pl.BlockSpec(memory_space=pl.ANY)]
        args += [in_vmem(prev), old]
        aliases = {len(args) - 1: 0}
    if with_slots:
        in_specs.append(pl.BlockSpec(memory_space=pltpu.SMEM))
        args.append(owner)
        out_specs.append(whole)
        out_shape.append(pltpu.VMEM((LON_BLOCKS // 2, 6, ROWS, LANES), F32))
        scratch += [
            pltpu.SMEM((LON_BLOCKS,), jnp.int32),
            pltpu.SMEM((LON_BLOCKS // 2,), jnp.int32),
        ]
    steps = groups // width

    def kernel(*refs):
        refs = list(refs)
        fixed, refs = refs[:8], refs[8:]
        edge = refs.pop(0) if with_edge else None
        before = refs.pop(0) if with_prev else None
        former = refs.pop(0) if with_prev else None
        owners = refs.pop(0) if with_slots else None
        result = refs.pop(0)
        acc = None if with_slots else refs.pop(0)
        windows = refs.pop(0) if with_edge and with_prev else None
        sent = refs.pop(0) if with_slots else None
        parts = refs.pop(0)
        if with_slots:
            acc = refs.pop(0)
        if with_edge and not with_prev:
            windows = refs.pop(0)
        finish_kernel(
            base,
            groups,
            width,
            *fixed,
            edge,
            before,
            former,
            result,
            acc,
            windows,
            parts,
        )
        if with_slots:

            @pl.when(pl.program_id(0) == steps - 1)
            def _():
                slots_kernel(owners, acc, sent, *refs)

    return pl.pallas_call(
        kernel,
        grid_spec=pltpu.PrefetchScalarGridSpec(
            num_scalar_prefetch=1,
            grid=(steps,),
            in_specs=in_specs,
            out_specs=out_specs,
            scratch_shapes=scratch,
        ),
        out_shape=out_shape,
        input_output_aliases=aliases,
        compiler_params=pltpu.CompilerParams(vmem_limit_bytes=LIMIT),
        name=name,
    )(*args)


def shards(spectrum, sea_mask, ice_mask, friction, wind_dir, ocean_owner):
    count = lax.axis_size("tiles")
    first_row = (lax.axis_index("tiles") * ROWS).astype(jnp.int32).reshape(1)
    spectral = in_hbm(spectrum.reshape(NF, NDIR, ROWS, NLON))
    sea = in_hbm(sea_mask)
    odd = lax.axis_index("tiles") % 2
    odd = odd.astype(jnp.int32).reshape(1)
    even = 1 - odd

    def swap(x, start):
        pairs = [(i, i + 1) for i in range(start, count - 1, 2)]
        return lax.ppermute(x, "tiles", pairs + [(j, i) for i, j in pairs])

    near = pack(even, spectral, sea, 0, GROUPS, 3, True, "near")
    sea, _ = lax.optimization_barrier((sea, near))
    near = swap(near, 0)
    far1 = pack(odd, spectral, sea, 0, G1, 1, True, "far1")
    sea, _ = lax.optimization_barrier((sea, far1))
    far1 = swap(far1, 1)
    far2 = pack(odd, spectral, sea, G1, G2, 1, False, "far2")
    far2 = swap(far2, 1)

    place = np.tile(np.arange(NF), 2)
    speeds = np.arange(2 * NF) < NF
    freq_pos = (lax.axis_index("bins") * NF + place).astype(F32)
    power = jnp.where(speeds, -freq_pos, freq_pos - (NFREQ - 1))
    table = jnp.power(jnp.where(speeds, 1.1, 1.03).astype(F32), power)
    table = table * jnp.where(speeds, COURANT_MAX, 1.0).astype(F32)
    trig = jnp.asarray(TRIG)

    own, mask, wind, metric = own_rows(
        spectral,
        table,
        trig,
        first_row,
        count * ROWS,
        sea,
        ice_mask,
        friction,
        wind_dir,
    )
    common = (table, trig, metric)
    out, acc = finish(
        odd, *common, mask, wind, own, near, None, None, None, 0, 3, "finish_near"
    )
    out, acc, windows = finish(
        even, *common, mask, wind, own, far1, acc, out, None, 0, 1, "finish_far1"
    )
    out, sent = finish(
        even,
        *common,
        windows,
        wind,
        own,
        far2,
        acc,
        out,
        ocean_owner,
        G1,
        1,
        "finish_far2",
    )

    got = lax.all_to_all(sent, "bins", 0, 0, tiled=True)
    total = got.sum(0)
    rest = total[4:].reshape(2, ROWS, 2, LANES // 2).transpose(0, 2, 1, 3)
    rest = rest.reshape(4, ROWS, LANES // 2)[:, :, : 2 * BLK - LANES]
    fields = jnp.concatenate([total[:4], rest], axis=2).reshape(4, ROWS, 2, BLK)
    return out.reshape(spectrum.shape), fields[:2], fields[2:]


def solution(mesh):
    field = P("tiles", None)
    blocks = P(None, "tiles", "bins", None)
    whole = P("bins", "tiles", None)
    return jax.shard_map(
        shards,
        mesh=mesh,
        in_specs=(whole, field, field, field, field, field),
        out_specs=(whole, blocks, blocks),
        check_vma=False,
    )
```

```python
import math

import jax
import jax.numpy as jnp
import numpy as np
from jax import lax
from jax.experimental import pallas as pl
from jax.experimental.pallas import tpu as pltpu
from jax.sharding import PartitionSpec as P

NDIR = 36
NFREQ = 32
LON_BLOCKS = 16
STEPS = 4
COURANT_MAX = 0.6
GRID_STEP = 0.25 * math.pi / 180.0

ROWS = 8
NLON = 1440
BLK = 90
LANES = 128
TILES = 12
TAIL = NLON - (TILES - 1) * LANES
NF = 4
GROUPS = 9
G1 = 6
G2 = GROUPS - G1
TPG = NF * (TILES - 1) + 1

F32 = jnp.float32
PER_STEP = 2
LIMIT = 16 << 20
ANGLES = (np.arange(NDIR, dtype=np.float32) + 0.5) * np.float32(2.0 * math.pi / NDIR)
TRIG = np.concatenate([np.cos(ANGLES), np.sin(ANGLES)]).astype(np.float32)


def lane_iota():
    return lax.broadcasted_iota(jnp.int32, (ROWS, LANES), 1)


def sub_iota():
    return lax.broadcasted_iota(jnp.int32, (ROWS, LANES), 0)


def pack_group(src_ref, local, mask_ref, out_ref, group, upward, lane, low):
    def pair(j, i):
        cols = pl.ds(i * LANES, LANES)
        mask = mask_ref[:, cols].astype(F32)
        first = src_ref[j, 2 * local, :, cols] * mask
        second = src_ref[j, 2 * local + 1, :, cols] * mask
        if upward:
            return jnp.where(low, pltpu.roll(first, 4, 0), second)
        return jnp.where(low, first, pltpu.roll(second, 4, 0))

    for i in range(TILES - 1):
        for j in range(NF):
            out_ref[group, j * (TILES - 1) + i] = pair(j, i)
    tail = pair(0, TILES - 1)
    for j in range(1, NF):
        moved = pltpu.roll(pair(j, TILES - 1), TAIL * j, 1)
        tail = jnp.where(lane >= TAIL * j, moved, tail)
    out_ref[group, TPG - 1] = tail


def pack_kernel(base, width, with_mask, up_ref, src_ref, mask_ref, out_ref):
    lane = lane_iota()
    low = sub_iota() < 4
    upward = up_ref[0] == 1

    def fill(is_up):
        for u in range(width):
            g = pl.program_id(0) * width + u
            local = u if is_up else width - 1 - u
            pack_group(src_ref, local, mask_ref, out_ref, g, is_up, lane, low)
            if with_mask:
                start = jnp.minimum(g, TILES // 2 - 1) * (2 * LANES)
                start = pl.multiple_of(start, 2 * LANES)
                first = mask_ref[:, pl.ds(start, LANES)].astype(F32)
                second = mask_ref[:, pl.ds(start + LANES, LANES)].astype(F32)
                if is_up:
                    first = pltpu.roll(first, 4, 0)
                else:
                    second = pltpu.roll(second, 4, 0)
                out_ref[g, TPG] = jnp.where(low, first, second)

    pl.when(upward)(lambda: fill(True))
    pl.when(jnp.logical_not(upward))(lambda: fill(False))


def block_of(base, width, step, south):
    last = (2 * GROUPS - base) // width - 1
    return jnp.where(south == 1, base // width + step, last - step)


def pack(upward, spectral, sea_mask, base, groups, width, with_mask, name):
    tiles = TPG + 1 if with_mask else TPG
    block = (NF, 2 * width, ROWS, TILES * LANES)
    return pl.pallas_call(
        lambda *refs: pack_kernel(base, width, with_mask, *refs),
        grid_spec=pltpu.PrefetchScalarGridSpec(
            num_scalar_prefetch=1,
            grid=(groups // width,),
            in_specs=[
                pl.BlockSpec(
                    block, lambda g, up: (0, block_of(base, width, g, up[0]), 0, 0)
                ),
                pl.BlockSpec((ROWS, TILES * LANES), lambda g, up: (0, 0)),
            ],
            out_specs=pl.BlockSpec(memory_space=pltpu.VMEM),
        ),
        out_shape=pltpu.VMEM((groups, tiles, ROWS, LANES), F32),
        compiler_params=pltpu.CompilerParams(vmem_limit_bytes=LIMIT),
        name=name,
    )(upward, spectral, sea_mask)


WEST, EAST, BOTH = 0, 1, 2


def fill_wrap(tiles, lane):
    last = tiles[-1]
    after = pltpu.roll(tiles[0], TAIL, 1)
    before = pltpu.roll(last, LANES - TAIL, 1)
    filled = jnp.where(lane < LANES - TAIL, after, before)
    return tiles[:-1] + [jnp.where(lane < TAIL, last, filled)]


def shift_lanes(tiles, west, lane):
    if west:
        moved = [pltpu.roll(t, 1, 1) for t in tiles]
        return [jnp.where(lane == 0, moved[i - 1], moved[i]) for i in range(TILES)]
    moved = [pltpu.roll(t, LANES - 1, 1) for t in tiles]
    return [
        jnp.where(lane == LANES - 1, moved[(i + 1) % TILES], moved[i])
        for i in range(TILES)
    ]


def x_side(direction):
    west = direction < NDIR // 4 or direction >= NDIR - NDIR // 4
    return WEST if west else EAST


def pair_side(dp):
    first, second = x_side(2 * dp), x_side(2 * dp + 1)
    return first if first == second else BOTH


def run_cases(index, values, south_below, side_of, body):
    found = {}
    for v in values:
        found.setdefault((v < south_below, side_of(v)), []).append(v)
    for (south, side), members in sorted(found.items()):
        cond = index == members[0]
        for m in members[1:]:
            cond = jnp.logical_or(cond, index == m)
        pl.when(cond)(lambda south=south, side=side: body(south, side))


def load_tiles(ref):
    return [ref[:, pl.ds(i * LANES, LANES)].astype(F32) for i in range(TILES)]


def fill_metric(first_row, lat_total, out_ref):
    sub = sub_iota()
    part = sub % 4
    rows = [(sub, sub >= 0)]
    rows += [(part - 4 + k, part < 3) for k in range(1, STEPS + 1)]
    rows += [(part + ROWS - k, part > 0) for k in range(1, STEPS + 1)]
    edge = math.cos((lat_total / 2 - 0.5) * GRID_STEP)
    for n, (row, inside) in enumerate(rows):
        row = (first_row + row).astype(F32)
        latitude = (row - lat_total / 2 + 0.5) * GRID_STEP
        out_ref[n] = jnp.where(inside, edge / jnp.cos(latitude), 0.0)


def own_kernel(
    lat_total,
    tab_ref,
    trig_ref,
    row_ref,
    sea_ref,
    ice_ref,
    friction_ref,
    wind_ref,
    src_ref,
    out_ref,
    mask_ref,
    force_ref,
    met_ref,
):
    step = pl.program_id(0)
    lane = lane_iota()
    sub = sub_iota()

    @pl.when(step == 0)
    def _():
        sea = fill_wrap(load_tiles(sea_ref), lane)
        ice = load_tiles(ice_ref)
        friction = load_tiles(friction_ref)
        wind = load_tiles(wind_ref)
        for i in range(TILES):
            strength = 0.5 * friction[i] * friction[i]
            mask_ref[i] = sea[i]
            force_ref[0, i] = strength * jnp.cos(wind[i])
            force_ref[1, i] = strength * jnp.sin(wind[i])
            force_ref[2, i] = 1.0 - 0.5 * ice[i]
        fill_metric(row_ref[0], lat_total, met_ref)

    def one(local, carry):
        direction = 2 * PER_STEP * step + local

        def body(south, side):
            west = side == WEST
            inflow = sub > 0 if south else sub < ROWS - 1
            fields = []
            coefs = []
            for j in range(NF):
                cy = tab_ref[j] * jnp.abs(trig_ref[NDIR + direction])
                cx = tab_ref[j] * jnp.abs(trig_ref[direction]) * met_ref[0]
                alpha = 1.0 - cx - cy
                coefs.append((alpha, cx, jnp.where(inflow, cy, 0.0)))
                tiles = [
                    src_ref[j, local, :, pl.ds(i * LANES, LANES)] for i in range(TILES)
                ]
                tiles = fill_wrap(tiles, lane)
                fields.append([t * mask_ref[i] for i, t in enumerate(tiles)])
            for sub_step in range(STEPS):
                new = []
                for tiles, (alpha, cx, cy) in zip(fields, coefs):
                    xs = shift_lanes(tiles, west, lane)
                    done = []
                    for i in range(TILES):
                        y = pltpu.roll(tiles[i], 1 if south else ROWS - 1, 0)
                        total = alpha * tiles[i] + cx * xs[i] + cy * y
                        done.append(total * mask_ref[i])
                    new.append(done)
                fields = new
            for j in range(NF):
                for i in range(TILES):
                    out_ref[local // 2, local % 2, j, i] = fields[j][i]

        run_cases(direction, range(NDIR), NDIR // 2, x_side, body)
        return carry

    lax.fori_loop(0, 2 * PER_STEP, one, 0)


def own_rows(
    spectral, table, trig, first_row, lat_total, sea_mask, ice_mask, friction, wind_dir
):
    whole = pl.BlockSpec(memory_space=pltpu.VMEM)
    field = pl.BlockSpec((ROWS, TILES * LANES), lambda i: (0, 0))
    return pl.pallas_call(
        lambda *refs: own_kernel(lat_total, *refs),
        grid=(2 * GROUPS // PER_STEP,),
        in_specs=[
            pl.BlockSpec(memory_space=pltpu.SMEM),
            pl.BlockSpec(memory_space=pltpu.SMEM),
            pl.BlockSpec(memory_space=pltpu.SMEM),
            field,
            field,
            field,
            field,
            pl.BlockSpec(
                (NF, 2 * PER_STEP, ROWS, TILES * LANES), lambda i: (0, i, 0, 0)
            ),
        ],
        out_specs=[
            pl.BlockSpec(
                (PER_STEP, 2, NF, TILES, ROWS, LANES), lambda i: (i, 0, 0, 0, 0, 0)
            ),
            whole,
            whole,
            whole,
        ],
        out_shape=[
            jax.ShapeDtypeStruct((2 * GROUPS, 2, NF, TILES, ROWS, LANES), F32),
            pltpu.VMEM((TILES, ROWS, LANES), F32),
            pltpu.VMEM((3, TILES, ROWS, LANES), F32),
            pltpu.VMEM((1 + 2 * STEPS, ROWS, LANES), F32),
        ],
        compiler_params=pltpu.CompilerParams(vmem_limit_bytes=LIMIT),
        name="own",
    )(table, trig, first_row, sea_mask, ice_mask, friction, wind_dir, spectral)


def window_masks(south, mask_ref, halo_ref, out_ref, lane, low):
    rows = []
    for i in range(TILES):
        edge = halo_ref[i // 2, 0]
        if (i % 2 == 0) != south:
            edge = pltpu.roll(edge, 4, 0)
        mine = pltpu.roll(mask_ref[i], 4, 0)
        if south:
            rows.append(jnp.where(low, edge, mine))
        else:
            rows.append(jnp.where(low, mine, edge))
    rows = fill_wrap(rows, lane)
    for k in range(1, STEPS + 1):
        first = k if south else 4 - k
        for i in range(TILES):
            window = rows[i]
            if first > 0:
                window = pltpu.roll(window, ROWS - first, 0)
            out_ref[k - 1, i] = jnp.where(low, window, pltpu.roll(window, 4, 0))


def finish_kernel(
    base,
    groups,
    width,
    south_ref,
    tab_ref,
    trig_ref,
    met_ref,
    mask_ref,
    wind_ref,
    own_ref,
    halo_ref,
    edge_ref,
    prev_ref,
    old_ref,
    out_ref,
    acc_ref,
    win_ref,
    c_ref,
):
    step = pl.program_id(0)
    is_south = south_ref[0] == 1
    dps = [base + g for g in range(groups)]
    dps = dps + [2 * GROUPS - 1 - d for d in dps]
    lane = lane_iota()
    sub = sub_iota()
    low = sub < 4

    @pl.when(step == 0)
    def _():
        if prev_ref is None:
            acc_ref[...] = jnp.zeros_like(acc_ref)
        else:
            acc_ref[...] = prev_ref[...]

    if edge_ref is not None:
        for south in (True, False):
            mine = jnp.logical_and(step == 0, is_south == south)
            pl.when(mine)(
                lambda south=south: window_masks(
                    south, mask_ref, edge_ref, win_ref, lane, low
                )
            )

    windows = mask_ref if edge_ref is None else win_ref

    def one(u, carry):
        local = jnp.where(is_south, u, width - 1 - u)
        group = base + step * width + u
        dp = jnp.where(is_south, group, 2 * GROUPS - 1 - group)

        def contribution(south, side):
            row = 0 if south else 1
            fields = []
            scalars = []
            for j in range(NF):
                courant = tab_ref[j]
                bx = courant * jnp.abs(
                    jnp.where(low, trig_ref[2 * dp], trig_ref[2 * dp + 1])
                )
                cy = courant * jnp.abs(
                    jnp.where(low, trig_ref[NDIR + 2 * dp], trig_ref[NDIR + 2 * dp + 1])
                )
                inside = sub % 4 < 3 if south else sub % 4 > 0
                scalars.append((bx, cy, jnp.where(inside, 1.0 - cy, 0.0)))
                tiles = [halo_ref[u, j * (TILES - 1) + i] for i in range(TILES - 1)]
                last = halo_ref[u, TPG - 1]
                if j > 0:
                    last = pltpu.roll(last, LANES - TAIL * j, 1)
                fields.append(fill_wrap(tiles + [last], lane))
            for k in range(STEPS):
                new = []
                for tiles, (bx, cy, rest) in zip(fields, scalars):
                    cx = bx * met_ref[1 + row * STEPS + k]
                    alpha = rest - cx
                    ahead = [pltpu.roll(t, ROWS - 1 if south else 1, 0) for t in tiles]
                    if side == BOTH:
                        west = shift_lanes(ahead, True, lane)
                        east = shift_lanes(ahead, False, lane)
                        here = low if south else jnp.logical_not(low)
                        xs = [jnp.where(here, w, e) for w, e in zip(west, east)]
                    else:
                        xs = shift_lanes(ahead, side == WEST, lane)
                    new.append(
                        [
                            (alpha * ahead[i] + cx * xs[i] + cy * tiles[i])
                            * windows[k, i]
                            for i in range(TILES)
                        ]
                    )
                fields = new
            for j in range(NF):
                for i in range(TILES):
                    c_ref[j, i] = fields[j][i]

        run_cases(dp, dps, GROUPS, pair_side, contribution)

        def combine(south, side):
            weight = [tab_ref[NF + j] for j in range(NF)]
            angle = [
                (trig_ref[2 * dp + dd], trig_ref[NDIR + 2 * dp + dd]) for dd in range(2)
            ]
            target = low if south else jnp.logical_not(low)
            for first in range(0, TILES, 2):
                held = []
                for i in (first, first + 1):
                    held.append(
                        (
                            [wind_ref[n, i] for n in range(3)],
                            [c_ref[j, i] for j in range(NF)],
                            [acc_ref[n, i] for n in range(4)],
                            [
                                [own_ref[local, dd, j, i] for j in range(NF)]
                                for dd in range(2)
                            ],
                        )
                    )
                results = []
                for (east, north, ice), parts, total, own in held:
                    made = []
                    for dd in range(2):
                        cos_d, sin_d = angle[dd]
                        h = jnp.maximum(cos_d * east + sin_d * north, 0.0)
                        for j in range(NF):
                            c = parts[j]
                            if (dd == 0) != south:
                                c = pltpu.roll(c, 4, 0)
                            e = own[dd][j] + jnp.where(target, c, 0.0)
                            x = weight[j] * e
                            made.append((e + h * x) * ice)
                            y = weight[j] * x
                            sum_x = x if j == 0 else sum_x + x
                            sum_y = y if j == 0 else sum_y + y
                        source = h * sum_x
                        drift = ice * (sum_x + h * sum_y)
                        total = [
                            total[0] + cos_d * drift,
                            total[1] + sin_d * drift,
                            total[2] + cos_d * source,
                            total[3] + sin_d * source,
                        ]
                    results.append((made, total))
                for i, (made, total) in zip((first, first + 1), results):
                    cols = pl.ds(i * LANES, LANES)
                    for dd in range(2):
                        for j in range(NF):
                            out_ref[j, 2 * local + dd, :, cols] = made[dd * NF + j]
                    for n in range(4):
                        acc_ref[n, i] = total[n]

        run_cases(dp, dps, GROUPS, lambda d: WEST, combine)
        return carry

    lax.fori_loop(0, width, one, 0)


def slots_kernel(owner_ref, acc_ref, out_ref, order_ref, count_ref):
    lane = lane_iota()
    for k in range(LON_BLOCKS // 2):
        count_ref[k] = 0
    for block in range(LON_BLOCKS):
        owner = owner_ref[0, block]
        seen = count_ref[owner]
        order_ref[2 * owner + seen] = block
        count_ref[owner] = seen + 1

    for k in range(LON_BLOCKS // 2):
        rests = []
        for c in range(4):
            parts = []
            for s in range(2):
                column = order_ref[2 * k + s] * BLK
                tile = column // LANES
                shift = column % LANES
                back = (LANES - shift) % LANES
                here = pltpu.roll(acc_ref[c, tile], back, 1)
                after = pltpu.roll(acc_ref[c, jnp.minimum(tile + 1, TILES - 1)], back, 1)
                parts.append(jnp.where(lane < LANES - shift, here, after))
            moved = pltpu.roll(parts[1], BLK, 1)
            out_ref[k, c] = jnp.where(lane < BLK, parts[0], moved)
            rests.append(moved)
        for c in range(2):
            other = pltpu.roll(rests[2 * c + 1], LANES // 2, 1)
            both = jnp.where(lane < LANES // 2, rests[2 * c], other)
            used = lane % (LANES // 2) < 2 * BLK - LANES
            out_ref[k, 4 + c] = jnp.where(used, both, 0.0)


def in_vmem(x):
    return pltpu.with_memory_space_constraint(x, pltpu.VMEM)


def in_hbm(x):
    return pltpu.with_memory_space_constraint(x, pltpu.HBM)


def finish(
    south,
    table,
    trig,
    metric,
    mask,
    wind,
    own,
    halo,
    prev,
    old,
    owner,
    base,
    width,
    name,
):
    groups, tiles = halo.shape[:2]
    whole = pl.BlockSpec(memory_space=pltpu.VMEM)
    block = lambda i, s: block_of(base, width, i, s[0])
    in_specs = [
        pl.BlockSpec(memory_space=pltpu.SMEM),
        pl.BlockSpec(memory_space=pltpu.SMEM),
        whole,
        whole,
        whole,
        pl.BlockSpec(
            (width, 2, NF, TILES, ROWS, LANES),
            lambda i, s: (block(i, s), 0, 0, 0, 0, 0),
        ),
        pl.BlockSpec((width, tiles, ROWS, LANES), lambda i, s: (i, 0, 0, 0)),
    ]
    halo = in_hbm(halo)
    args = [south, table, trig, in_vmem(metric), in_vmem(mask), in_vmem(wind)]
    args += [own, halo]
    out_specs = [
        pl.BlockSpec(
            (NF, 2 * width, ROWS, TILES * LANES), lambda i, s: (0, block(i, s), 0, 0)
        )
    ]
    out_shape = [jax.ShapeDtypeStruct((NF, NDIR, ROWS, NLON), F32)]
    acc_type = pltpu.VMEM((4, TILES, ROWS, LANES), F32)
    window_type = pltpu.VMEM((STEPS, TILES, ROWS, LANES), F32)
    scratch = [pltpu.VMEM((NF, TILES, ROWS, LANES), F32)]
    with_slots = owner is not None
    if with_slots:
        scratch.append(acc_type)
    else:
        out_specs.append(whole)
        out_shape.append(acc_type)
    with_edge = tiles > TPG
    with_prev = prev is not None
    aliases = {}
    if with_edge:
        in_specs.append(
            pl.BlockSpec((TILES // 2, 1, ROWS, LANES), lambda i, s: (0, TPG, 0, 0))
        )
        args.append(halo)
        if with_prev:
            out_specs.append(whole)
            out_shape.append(window_type)
        else:
            scratch.append(window_type)
    if with_prev:
        in_specs += [whole, pl.BlockSpec(memory_space=pl.ANY)]
        args += [in_vmem(prev), old]
        aliases = {len(args) - 1: 0}
    if with_slots:
        in_specs.append(pl.BlockSpec(memory_space=pltpu.SMEM))
        args.append(owner)
        out_specs.append(whole)
        out_shape.append(pltpu.VMEM((LON_BLOCKS // 2, 6, ROWS, LANES), F32))
        scratch += [
            pltpu.SMEM((LON_BLOCKS,), jnp.int32),
            pltpu.SMEM((LON_BLOCKS // 2,), jnp.int32),
        ]
    steps = groups // width

    def kernel(*refs):
        refs = list(refs)
        fixed, refs = refs[:8], refs[8:]
        edge = refs.pop(0) if with_edge else None
        before = refs.pop(0) if with_prev else None
        former = refs.pop(0) if with_prev else None
        owners = refs.pop(0) if with_slots else None
        result = refs.pop(0)
        acc = None if with_slots else refs.pop(0)
        windows = refs.pop(0) if with_edge and with_prev else None
        sent = refs.pop(0) if with_slots else None
        parts = refs.pop(0)
        if with_slots:
            acc = refs.pop(0)
        if with_edge and not with_prev:
            windows = refs.pop(0)
        finish_kernel(
            base,
            groups,
            width,
            *fixed,
            edge,
            before,
            former,
            result,
            acc,
            windows,
            parts,
        )
        if with_slots:

            @pl.when(pl.program_id(0) == steps - 1)
            def _():
                slots_kernel(owners, acc, sent, *refs)

    return pl.pallas_call(
        kernel,
        grid_spec=pltpu.PrefetchScalarGridSpec(
            num_scalar_prefetch=1,
            grid=(steps,),
            in_specs=in_specs,
            out_specs=out_specs,
            scratch_shapes=scratch,
        ),
        out_shape=out_shape,
        input_output_aliases=aliases,
        compiler_params=pltpu.CompilerParams(vmem_limit_bytes=LIMIT),
        name=name,
    )(*args)


def shards(spectrum, sea_mask, ice_mask, friction, wind_dir, ocean_owner):
    count = lax.axis_size("tiles")
    first_row = (lax.axis_index("tiles") * ROWS).astype(jnp.int32).reshape(1)
    spectral = in_hbm(spectrum.reshape(NF, NDIR, ROWS, NLON))
    sea = in_hbm(sea_mask)
    odd = lax.axis_index("tiles") % 2
    odd = odd.astype(jnp.int32).reshape(1)
    even = 1 - odd

    def swap(x, start):
        pairs = [(i, i + 1) for i in range(start, count - 1, 2)]
        return lax.ppermute(x, "tiles", pairs + [(j, i) for i, j in pairs])

    near = pack(even, spectral, sea, 0, GROUPS, 3, True, "near")
    sea, _ = lax.optimization_barrier((sea, near))
    near = swap(near, 0)
    far1 = pack(odd, spectral, sea, 0, G1, 2, True, "far1")
    sea, _ = lax.optimization_barrier((sea, far1))
    far1 = swap(far1, 1)
    far2 = pack(odd, spectral, sea, G1, G2, 3, False, "far2")
    far2 = swap(far2, 1)

    place = np.tile(np.arange(NF), 2)
    speeds = np.arange(2 * NF) < NF
    freq_pos = (lax.axis_index("bins") * NF + place).astype(F32)
    power = jnp.where(speeds, -freq_pos, freq_pos - (NFREQ - 1))
    table = jnp.power(jnp.where(speeds, 1.1, 1.03).astype(F32), power)
    table = table * jnp.where(speeds, COURANT_MAX, 1.0).astype(F32)
    trig = jnp.asarray(TRIG)

    own, mask, wind, metric = own_rows(
        spectral,
        table,
        trig,
        first_row,
        count * ROWS,
        sea,
        ice_mask,
        friction,
        wind_dir,
    )
    common = (table, trig, metric)
    out, acc = finish(
        odd, *common, mask, wind, own, near, None, None, None, 0, 3, "finish_near"
    )
    out, acc, windows = finish(
        even, *common, mask, wind, own, far1, acc, out, None, 0, 2, "finish_far1"
    )
    out, sent = finish(
        even,
        *common,
        windows,
        wind,
        own,
        far2,
        acc,
        out,
        ocean_owner,
        G1,
        1,
        "finish_far2",
    )

    got = lax.all_to_all(sent, "bins", 0, 0, tiled=True)
    total = got.sum(0)
    rest = total[4:].reshape(2, ROWS, 2, LANES // 2).transpose(0, 2, 1, 3)
    rest = rest.reshape(4, ROWS, LANES // 2)[:, :, : 2 * BLK - LANES]
    fields = jnp.concatenate([total[:4], rest], axis=2).reshape(4, ROWS, 2, BLK)
    return out.reshape(spectrum.shape), fields[:2], fields[2:]


def solution(mesh):
    field = P("tiles", None)
    blocks = P(None, "tiles", "bins", None)
    whole = P("bins", "tiles", None)
    return jax.shard_map(
        shards,
        mesh=mesh,
        in_specs=(whole, field, field, field, field, field),
        out_specs=(whole, blocks, blocks),
        check_vma=False,
    )
```

```python
import math

import jax
import jax.numpy as jnp
import numpy as np
from jax import lax
from jax.experimental import pallas as pl
from jax.experimental.pallas import tpu as pltpu
from jax.sharding import PartitionSpec as P

NDIR = 36
NFREQ = 32
LON_BLOCKS = 16
STEPS = 4
COURANT_MAX = 0.6
GRID_STEP = 0.25 * math.pi / 180.0

ROWS = 8
NLON = 1440
BLK = 90
LANES = 128
TILES = 12
TAIL = NLON - (TILES - 1) * LANES
NF = 4
GROUPS = 9
G1 = 6
G2 = GROUPS - G1
TPG = NF * (TILES - 1) + 1

F32 = jnp.float32
PER_STEP = 2
LIMIT = 16 << 20
ANGLES = (np.arange(NDIR, dtype=np.float32) + 0.5) * np.float32(2.0 * math.pi / NDIR)
TRIG = np.concatenate([np.cos(ANGLES), np.sin(ANGLES)]).astype(np.float32)


def lane_iota():
    return lax.broadcasted_iota(jnp.int32, (ROWS, LANES), 1)


def sub_iota():
    return lax.broadcasted_iota(jnp.int32, (ROWS, LANES), 0)


def pack_group(src_ref, local, mask_ref, out_ref, group, upward, lane, low):
    def pair(j, i):
        cols = pl.ds(i * LANES, LANES)
        mask = mask_ref[:, cols].astype(F32)
        first = src_ref[j, 2 * local, :, cols] * mask
        second = src_ref[j, 2 * local + 1, :, cols] * mask
        if upward:
            return jnp.where(low, pltpu.roll(first, 4, 0), second)
        return jnp.where(low, first, pltpu.roll(second, 4, 0))

    for i in range(TILES - 1):
        for j in range(NF):
            out_ref[group, j * (TILES - 1) + i] = pair(j, i)
    tail = pair(0, TILES - 1)
    for j in range(1, NF):
        moved = pltpu.roll(pair(j, TILES - 1), TAIL * j, 1)
        tail = jnp.where(lane >= TAIL * j, moved, tail)
    out_ref[group, TPG - 1] = tail


def pack_kernel(base, width, with_mask, up_ref, src_ref, mask_ref, out_ref):
    lane = lane_iota()
    low = sub_iota() < 4
    upward = up_ref[0] == 1

    def fill(is_up):
        for u in range(width):
            g = pl.program_id(0) * width + u
            local = u if is_up else width - 1 - u
            pack_group(src_ref, local, mask_ref, out_ref, g, is_up, lane, low)
            if with_mask:
                start = jnp.minimum(g, TILES // 2 - 1) * (2 * LANES)
                start = pl.multiple_of(start, 2 * LANES)
                first = mask_ref[:, pl.ds(start, LANES)].astype(F32)
                second = mask_ref[:, pl.ds(start + LANES, LANES)].astype(F32)
                if is_up:
                    first = pltpu.roll(first, 4, 0)
                else:
                    second = pltpu.roll(second, 4, 0)
                out_ref[g, TPG] = jnp.where(low, first, second)

    pl.when(upward)(lambda: fill(True))
    pl.when(jnp.logical_not(upward))(lambda: fill(False))


def block_of(base, width, step, south):
    last = (2 * GROUPS - base) // width - 1
    return jnp.where(south == 1, base // width + step, last - step)


def pack(upward, spectral, sea_mask, base, groups, width, with_mask, name):
    tiles = TPG + 1 if with_mask else TPG
    block = (NF, 2 * width, ROWS, TILES * LANES)
    return pl.pallas_call(
        lambda *refs: pack_kernel(base, width, with_mask, *refs),
        grid_spec=pltpu.PrefetchScalarGridSpec(
            num_scalar_prefetch=1,
            grid=(groups // width,),
            in_specs=[
                pl.BlockSpec(
                    block, lambda g, up: (0, block_of(base, width, g, up[0]), 0, 0)
                ),
                pl.BlockSpec((ROWS, TILES * LANES), lambda g, up: (0, 0)),
            ],
            out_specs=pl.BlockSpec(memory_space=pltpu.VMEM),
        ),
        out_shape=pltpu.VMEM((groups, tiles, ROWS, LANES), F32),
        compiler_params=pltpu.CompilerParams(vmem_limit_bytes=LIMIT),
        name=name,
    )(upward, spectral, sea_mask)


WEST, EAST, BOTH = 0, 1, 2


def fill_wrap(tiles, lane):
    last = tiles[-1]
    after = pltpu.roll(tiles[0], TAIL, 1)
    before = pltpu.roll(last, LANES - TAIL, 1)
    filled = jnp.where(lane < LANES - TAIL, after, before)
    return tiles[:-1] + [jnp.where(lane < TAIL, last, filled)]


def shift_lanes(tiles, west, lane):
    if west:
        moved = [pltpu.roll(t, 1, 1) for t in tiles]
        return [jnp.where(lane == 0, moved[i - 1], moved[i]) for i in range(TILES)]
    moved = [pltpu.roll(t, LANES - 1, 1) for t in tiles]
    return [
        jnp.where(lane == LANES - 1, moved[(i + 1) % TILES], moved[i])
        for i in range(TILES)
    ]


def x_side(direction):
    west = direction < NDIR // 4 or direction >= NDIR - NDIR // 4
    return WEST if west else EAST


def pair_side(dp):
    first, second = x_side(2 * dp), x_side(2 * dp + 1)
    return first if first == second else BOTH


def run_cases(index, values, south_below, side_of, body):
    found = {}
    for v in values:
        found.setdefault((v < south_below, side_of(v)), []).append(v)
    for (south, side), members in sorted(found.items()):
        cond = index == members[0]
        for m in members[1:]:
            cond = jnp.logical_or(cond, index == m)
        pl.when(cond)(lambda south=south, side=side: body(south, side))


def load_tiles(ref):
    return [ref[:, pl.ds(i * LANES, LANES)].astype(F32) for i in range(TILES)]


def fill_metric(first_row, lat_total, out_ref):
    sub = sub_iota()
    part = sub % 4
    rows = [(sub, sub >= 0)]
    rows += [(part - 4 + k, part < 3) for k in range(1, STEPS + 1)]
    rows += [(part + ROWS - k, part > 0) for k in range(1, STEPS + 1)]
    edge = math.cos((lat_total / 2 - 0.5) * GRID_STEP)
    for n, (row, inside) in enumerate(rows):
        row = (first_row + row).astype(F32)
        latitude = (row - lat_total / 2 + 0.5) * GRID_STEP
        out_ref[n] = jnp.where(inside, edge / jnp.cos(latitude), 0.0)


def own_kernel(
    lat_total,
    tab_ref,
    trig_ref,
    row_ref,
    sea_ref,
    ice_ref,
    friction_ref,
    wind_ref,
    src_ref,
    out_ref,
    mask_ref,
    force_ref,
    met_ref,
):
    step = pl.program_id(0)
    lane = lane_iota()
    sub = sub_iota()

    @pl.when(step == 0)
    def _():
        sea = fill_wrap(load_tiles(sea_ref), lane)
        ice = load_tiles(ice_ref)
        friction = load_tiles(friction_ref)
        wind = load_tiles(wind_ref)
        for i in range(TILES):
            strength = 0.5 * friction[i] * friction[i]
            mask_ref[i] = sea[i]
            force_ref[0, i] = strength * jnp.cos(wind[i])
            force_ref[1, i] = strength * jnp.sin(wind[i])
            force_ref[2, i] = 1.0 - 0.5 * ice[i]
        fill_metric(row_ref[0], lat_total, met_ref)

    def one(local, carry):
        direction = 2 * PER_STEP * step + local

        def body(south, side):
            west = side == WEST
            inflow = sub > 0 if south else sub < ROWS - 1
            fields = []
            coefs = []
            for j in range(NF):
                cy = tab_ref[j] * jnp.abs(trig_ref[NDIR + direction])
                cx = tab_ref[j] * jnp.abs(trig_ref[direction]) * met_ref[0]
                alpha = 1.0 - cx - cy
                coefs.append((alpha, cx, jnp.where(inflow, cy, 0.0)))
                tiles = [
                    src_ref[j, local, :, pl.ds(i * LANES, LANES)] for i in range(TILES)
                ]
                tiles = fill_wrap(tiles, lane)
                fields.append([t * mask_ref[i] for i, t in enumerate(tiles)])
            for sub_step in range(STEPS):
                new = []
                for tiles, (alpha, cx, cy) in zip(fields, coefs):
                    xs = shift_lanes(tiles, west, lane)
                    done = []
                    for i in range(TILES):
                        y = pltpu.roll(tiles[i], 1 if south else ROWS - 1, 0)
                        total = alpha * tiles[i] + cx * xs[i] + cy * y
                        done.append(total * mask_ref[i])
                    new.append(done)
                fields = new
            for j in range(NF):
                for i in range(TILES):
                    out_ref[local // 2, local % 2, j, i] = fields[j][i]

        run_cases(direction, range(NDIR), NDIR // 2, x_side, body)
        return carry

    lax.fori_loop(0, 2 * PER_STEP, one, 0)


def own_rows(
    spectral, table, trig, first_row, lat_total, sea_mask, ice_mask, friction, wind_dir
):
    whole = pl.BlockSpec(memory_space=pltpu.VMEM)
    field = pl.BlockSpec((ROWS, TILES * LANES), lambda i: (0, 0))
    return pl.pallas_call(
        lambda *refs: own_kernel(lat_total, *refs),
        grid=(2 * GROUPS // PER_STEP,),
        in_specs=[
            pl.BlockSpec(memory_space=pltpu.SMEM),
            pl.BlockSpec(memory_space=pltpu.SMEM),
            pl.BlockSpec(memory_space=pltpu.SMEM),
            field,
            field,
            field,
            field,
            pl.BlockSpec(
                (NF, 2 * PER_STEP, ROWS, TILES * LANES), lambda i: (0, i, 0, 0)
            ),
        ],
        out_specs=[
            pl.BlockSpec(
                (PER_STEP, 2, NF, TILES, ROWS, LANES), lambda i: (i, 0, 0, 0, 0, 0)
            ),
            whole,
            whole,
            whole,
        ],
        out_shape=[
            jax.ShapeDtypeStruct((2 * GROUPS, 2, NF, TILES, ROWS, LANES), F32),
            pltpu.VMEM((TILES, ROWS, LANES), F32),
            pltpu.VMEM((3, TILES, ROWS, LANES), F32),
            pltpu.VMEM((1 + 2 * STEPS, ROWS, LANES), F32),
        ],
        compiler_params=pltpu.CompilerParams(vmem_limit_bytes=LIMIT),
        name="own",
    )(table, trig, first_row, sea_mask, ice_mask, friction, wind_dir, spectral)


def window_masks(south, mask_ref, halo_ref, out_ref, lane, low):
    rows = []
    for i in range(TILES):
        edge = halo_ref[i // 2, 0]
        if (i % 2 == 0) != south:
            edge = pltpu.roll(edge, 4, 0)
        mine = pltpu.roll(mask_ref[i], 4, 0)
        if south:
            rows.append(jnp.where(low, edge, mine))
        else:
            rows.append(jnp.where(low, mine, edge))
    rows = fill_wrap(rows, lane)
    for k in range(1, STEPS + 1):
        first = k if south else 4 - k
        for i in range(TILES):
            window = rows[i]
            if first > 0:
                window = pltpu.roll(window, ROWS - first, 0)
            out_ref[k - 1, i] = jnp.where(low, window, pltpu.roll(window, 4, 0))


def finish_kernel(
    base,
    groups,
    width,
    south_ref,
    tab_ref,
    trig_ref,
    met_ref,
    mask_ref,
    wind_ref,
    own_ref,
    halo_ref,
    edge_ref,
    prev_ref,
    old_ref,
    out_ref,
    acc_ref,
    win_ref,
    c_ref,
):
    step = pl.program_id(0)
    is_south = south_ref[0] == 1
    dps = [base + g for g in range(groups)]
    dps = dps + [2 * GROUPS - 1 - d for d in dps]
    lane = lane_iota()
    sub = sub_iota()
    low = sub < 4

    @pl.when(step == 0)
    def _():
        if prev_ref is None:
            acc_ref[...] = jnp.zeros_like(acc_ref)
        else:
            acc_ref[...] = prev_ref[...]

    if edge_ref is not None:
        for south in (True, False):
            mine = jnp.logical_and(step == 0, is_south == south)
            pl.when(mine)(
                lambda south=south: window_masks(
                    south, mask_ref, edge_ref, win_ref, lane, low
                )
            )

    windows = mask_ref if edge_ref is None else win_ref

    def one(u, carry):
        local = jnp.where(is_south, u, width - 1 - u)
        group = base + step * width + u
        dp = jnp.where(is_south, group, 2 * GROUPS - 1 - group)

        def contribution(south, side):
            row = 0 if south else 1
            fields = []
            scalars = []
            for j in range(NF):
                courant = tab_ref[j]
                bx = courant * jnp.abs(
                    jnp.where(low, trig_ref[2 * dp], trig_ref[2 * dp + 1])
                )
                cy = courant * jnp.abs(
                    jnp.where(low, trig_ref[NDIR + 2 * dp], trig_ref[NDIR + 2 * dp + 1])
                )
                inside = sub % 4 < 3 if south else sub % 4 > 0
                scalars.append((bx, cy, jnp.where(inside, 1.0 - cy, 0.0)))
                tiles = [halo_ref[u, j * (TILES - 1) + i] for i in range(TILES - 1)]
                last = halo_ref[u, TPG - 1]
                if j > 0:
                    last = pltpu.roll(last, LANES - TAIL * j, 1)
                fields.append(fill_wrap(tiles + [last], lane))
            for k in range(STEPS):
                new = []
                for tiles, (bx, cy, rest) in zip(fields, scalars):
                    cx = bx * met_ref[1 + row * STEPS + k]
                    alpha = rest - cx
                    ahead = [pltpu.roll(t, ROWS - 1 if south else 1, 0) for t in tiles]
                    if side == BOTH:
                        west = shift_lanes(ahead, True, lane)
                        east = shift_lanes(ahead, False, lane)
                        here = low if south else jnp.logical_not(low)
                        xs = [jnp.where(here, w, e) for w, e in zip(west, east)]
                    else:
                        xs = shift_lanes(ahead, side == WEST, lane)
                    new.append(
                        [
                            (alpha * ahead[i] + cx * xs[i] + cy * tiles[i])
                            * windows[k, i]
                            for i in range(TILES)
                        ]
                    )
                fields = new
            for j in range(NF):
                for i in range(TILES):
                    c_ref[j, i] = fields[j][i]

        run_cases(dp, dps, GROUPS, pair_side, contribution)

        def combine(south, side):
            weight = [tab_ref[NF + j] for j in range(NF)]
            angle = [
                (trig_ref[2 * dp + dd], trig_ref[NDIR + 2 * dp + dd]) for dd in range(2)
            ]
            target = low if south else jnp.logical_not(low)
            for first in range(0, TILES, 2):
                held = []
                for i in (first, first + 1):
                    held.append(
                        (
                            [wind_ref[n, i] for n in range(3)],
                            [c_ref[j, i] for j in range(NF)],
                            [acc_ref[n, i] for n in range(4)],
                            [
                                [own_ref[local, dd, j, i] for j in range(NF)]
                                for dd in range(2)
                            ],
                        )
                    )
                results = []
                for (east, north, ice), parts, total, own in held:
                    made = []
                    for dd in range(2):
                        cos_d, sin_d = angle[dd]
                        h = jnp.maximum(cos_d * east + sin_d * north, 0.0)
                        for j in range(NF):
                            c = parts[j]
                            if (dd == 0) != south:
                                c = pltpu.roll(c, 4, 0)
                            e = own[dd][j] + jnp.where(target, c, 0.0)
                            x = weight[j] * e
                            made.append((e + h * x) * ice)
                            y = weight[j] * x
                            sum_x = x if j == 0 else sum_x + x
                            sum_y = y if j == 0 else sum_y + y
                        source = h * sum_x
                        drift = ice * (sum_x + h * sum_y)
                        total = [
                            total[0] + cos_d * drift,
                            total[1] + sin_d * drift,
                            total[2] + cos_d * source,
                            total[3] + sin_d * source,
                        ]
                    results.append((made, total))
                for i, (made, total) in zip((first, first + 1), results):
                    cols = pl.ds(i * LANES, LANES)
                    for dd in range(2):
                        for j in range(NF):
                            out_ref[j, 2 * local + dd, :, cols] = made[dd * NF + j]
                    for n in range(4):
                        acc_ref[n, i] = total[n]

        run_cases(dp, dps, GROUPS, lambda d: WEST, combine)
        return carry

    lax.fori_loop(0, width, one, 0)


def slots_kernel(owner_ref, acc_ref, out_ref, order_ref, count_ref):
    lane = lane_iota()
    for k in range(LON_BLOCKS // 2):
        count_ref[k] = 0
    for block in range(LON_BLOCKS):
        owner = owner_ref[0, block]
        seen = count_ref[owner]
        order_ref[2 * owner + seen] = block
        count_ref[owner] = seen + 1

    for k in range(LON_BLOCKS // 2):
        rests = []
        for c in range(4):
            parts = []
            for s in range(2):
                column = order_ref[2 * k + s] * BLK
                tile = column // LANES
                shift = column % LANES
                back = (LANES - shift) % LANES
                here = pltpu.roll(acc_ref[c, tile], back, 1)
                after = pltpu.roll(acc_ref[c, jnp.minimum(tile + 1, TILES - 1)], back, 1)
                parts.append(jnp.where(lane < LANES - shift, here, after))
            moved = pltpu.roll(parts[1], BLK, 1)
            out_ref[k, c] = jnp.where(lane < BLK, parts[0], moved)
            rests.append(moved)
        for c in range(2):
            other = pltpu.roll(rests[2 * c + 1], LANES // 2, 1)
            both = jnp.where(lane < LANES // 2, rests[2 * c], other)
            used = lane % (LANES // 2) < 2 * BLK - LANES
            out_ref[k, 4 + c] = jnp.where(used, both, 0.0)


def in_vmem(x):
    return pltpu.with_memory_space_constraint(x, pltpu.VMEM)


def in_hbm(x):
    return pltpu.with_memory_space_constraint(x, pltpu.HBM)


def finish(
    south,
    table,
    trig,
    metric,
    mask,
    wind,
    own,
    halo,
    prev,
    old,
    owner,
    base,
    width,
    name,
):
    groups, tiles = halo.shape[:2]
    whole = pl.BlockSpec(memory_space=pltpu.VMEM)
    block = lambda i, s: block_of(base, width, i, s[0])
    in_specs = [
        pl.BlockSpec(memory_space=pltpu.SMEM),
        pl.BlockSpec(memory_space=pltpu.SMEM),
        whole,
        whole,
        whole,
        pl.BlockSpec(
            (width, 2, NF, TILES, ROWS, LANES),
            lambda i, s: (block(i, s), 0, 0, 0, 0, 0),
        ),
        pl.BlockSpec((width, tiles, ROWS, LANES), lambda i, s: (i, 0, 0, 0)),
    ]
    halo = in_hbm(halo)
    args = [south, table, trig, in_vmem(metric), in_vmem(mask), in_vmem(wind)]
    args += [own, halo]
    out_specs = [
        pl.BlockSpec(
            (NF, 2 * width, ROWS, TILES * LANES), lambda i, s: (0, block(i, s), 0, 0)
        )
    ]
    out_shape = [jax.ShapeDtypeStruct((NF, NDIR, ROWS, NLON), F32)]
    acc_type = pltpu.VMEM((4, TILES, ROWS, LANES), F32)
    window_type = pltpu.VMEM((STEPS, TILES, ROWS, LANES), F32)
    scratch = [pltpu.VMEM((NF, TILES, ROWS, LANES), F32)]
    with_slots = owner is not None
    if with_slots:
        scratch.append(acc_type)
    else:
        out_specs.append(whole)
        out_shape.append(acc_type)
    with_edge = tiles > TPG
    with_prev = prev is not None
    aliases = {}
    if with_edge:
        in_specs.append(
            pl.BlockSpec((TILES // 2, 1, ROWS, LANES), lambda i, s: (0, TPG, 0, 0))
        )
        args.append(halo)
        if with_prev:
            out_specs.append(whole)
            out_shape.append(window_type)
        else:
            scratch.append(window_type)
    if with_prev:
        in_specs += [whole, pl.BlockSpec(memory_space=pl.ANY)]
        args += [in_vmem(prev), old]
        aliases = {len(args) - 1: 0}
    if with_slots:
        in_specs.append(pl.BlockSpec(memory_space=pltpu.SMEM))
        args.append(owner)
        out_specs.append(whole)
        out_shape.append(pltpu.VMEM((LON_BLOCKS // 2, 6, ROWS, LANES), F32))
        scratch += [
            pltpu.SMEM((LON_BLOCKS,), jnp.int32),
            pltpu.SMEM((LON_BLOCKS // 2,), jnp.int32),
        ]
    steps = groups // width

    def kernel(*refs):
        refs = list(refs)
        fixed, refs = refs[:8], refs[8:]
        edge = refs.pop(0) if with_edge else None
        before = refs.pop(0) if with_prev else None
        former = refs.pop(0) if with_prev else None
        owners = refs.pop(0) if with_slots else None
        result = refs.pop(0)
        acc = None if with_slots else refs.pop(0)
        windows = refs.pop(0) if with_edge and with_prev else None
        sent = refs.pop(0) if with_slots else None
        parts = refs.pop(0)
        if with_slots:
            acc = refs.pop(0)
        if with_edge and not with_prev:
            windows = refs.pop(0)
        finish_kernel(
            base,
            groups,
            width,
            *fixed,
            edge,
            before,
            former,
            result,
            acc,
            windows,
            parts,
        )
        if with_slots:

            @pl.when(pl.program_id(0) == steps - 1)
            def _():
                slots_kernel(owners, acc, sent, *refs)

    return pl.pallas_call(
        kernel,
        grid_spec=pltpu.PrefetchScalarGridSpec(
            num_scalar_prefetch=1,
            grid=(steps,),
            in_specs=in_specs,
            out_specs=out_specs,
            scratch_shapes=scratch,
        ),
        out_shape=out_shape,
        input_output_aliases=aliases,
        compiler_params=pltpu.CompilerParams(vmem_limit_bytes=LIMIT),
        name=name,
    )(*args)


def shards(spectrum, sea_mask, ice_mask, friction, wind_dir, ocean_owner):
    count = lax.axis_size("tiles")
    first_row = (lax.axis_index("tiles") * ROWS).astype(jnp.int32).reshape(1)
    spectral = in_hbm(spectrum.reshape(NF, NDIR, ROWS, NLON))
    sea = in_hbm(sea_mask)
    odd = lax.axis_index("tiles") % 2
    odd = odd.astype(jnp.int32).reshape(1)
    even = 1 - odd

    def swap(x, start):
        pairs = [(i, i + 1) for i in range(start, count - 1, 2)]
        return lax.ppermute(x, "tiles", pairs + [(j, i) for i, j in pairs])

    near = pack(even, spectral, sea, 0, GROUPS, 3, True, "near")
    sea, _ = lax.optimization_barrier((sea, near))
    near = swap(near, 0)
    far1 = pack(odd, spectral, sea, 0, G1, 3, True, "far1")
    sea, _ = lax.optimization_barrier((sea, far1))
    far1 = swap(far1, 1)
    far2 = pack(odd, spectral, sea, G1, G2, 3, False, "far2")
    far2 = swap(far2, 1)

    place = np.tile(np.arange(NF), 2)
    speeds = np.arange(2 * NF) < NF
    freq_pos = (lax.axis_index("bins") * NF + place).astype(F32)
    power = jnp.where(speeds, -freq_pos, freq_pos - (NFREQ - 1))
    table = jnp.power(jnp.where(speeds, 1.1, 1.03).astype(F32), power)
    table = table * jnp.where(speeds, COURANT_MAX, 1.0).astype(F32)
    trig = jnp.asarray(TRIG)

    own, mask, wind, metric = own_rows(
        spectral,
        table,
        trig,
        first_row,
        count * ROWS,
        sea,
        ice_mask,
        friction,
        wind_dir,
    )
    common = (table, trig, metric)
    out, acc = finish(
        odd, *common, mask, wind, own, near, None, None, None, 0, 3, "finish_near"
    )
    out, acc, windows = finish(
        even, *common, mask, wind, own, far1, acc, out, None, 0, 3, "finish_far1"
    )
    out, sent = finish(
        even,
        *common,
        windows,
        wind,
        own,
        far2,
        acc,
        out,
        ocean_owner,
        G1,
        1,
        "finish_far2",
    )

    got = lax.all_to_all(sent, "bins", 0, 0, tiled=True)
    total = got.sum(0)
    rest = total[4:].reshape(2, ROWS, 2, LANES // 2).transpose(0, 2, 1, 3)
    rest = rest.reshape(4, ROWS, LANES // 2)[:, :, : 2 * BLK - LANES]
    fields = jnp.concatenate([total[:4], rest], axis=2).reshape(4, ROWS, 2, BLK)
    return out.reshape(spectrum.shape), fields[:2], fields[2:]


def solution(mesh):
    field = P("tiles", None)
    blocks = P(None, "tiles", "bins", None)
    whole = P("bins", "tiles", None)
    return jax.shard_map(
        shards,
        mesh=mesh,
        in_specs=(whole, field, field, field, field, field),
        out_specs=(whole, blocks, blocks),
        check_vma=False,
    )
```
